128 devices in a mesh: pat: 2 (over x_lo), gx: 64 (over z, x_hi, y, core).
Axes of the slice: x: 4 (x_hi: 2, x_lo: 2; x = x_hi * 2 + x_lo), y: 4, z: 4, core: 2. Of those that a mesh axis runs over, the one named last changes fastest.
Arguments:
- pattern_index: int32 [2], P('pat'), may hold values from 0 to 7
- patterns: float32 [8, 512, 1024], P(None, 'gx'), may hold values from -6 to 6
- freq_bins: int32 [16], replicated, may hold values from 0 to 511
- absorption: float32 [512, 1024, 128], P('gx'), may hold values from 0.05 to 0.5
- forward_start: float32 [2, 512, 1024, 128], P('pat', 'gx'), may hold values from -6 to 6
- adjoint_start: float32 [2, 512, 1024, 128], P('pat', 'gx'), may hold values from -6 to 6
- measured: float32 [2, 2, 16, 1024], P('pat', None, None, 'gx'), may hold values from -6 to 6
Outputs:
- gradient: float32 [512, 1024, 128], P('gx', 'pat')
- model: float32 [2, 2, 16, 1024], P('pat', None, None, 'gx')
The draws below stay inside these ranges and needn't reach their ends.
All inputs are finite; a program needn't handle non-finite values.
Results may differ from the reference program's by a relative error of at most 0.00029.
Values sent between devices are 32-bit elements; how exact they have to be, the bound alone decides.
No kernel may reach another device: no remote copies, remote signals or barrier semaphores. Data moves between devices by JAX's collectives and lax.ppermute only.
A program may use at most 128 MiB of HBM per device.

```python
import math
import jax
import jax.numpy as jnp
from jax import lax

GROUPS = 2
NTABLE = 8
NX = 512
NY = 1024
NZ = 128
K = 16
SWEEPS = 4


def touch_ends(result, rng, least, largest):
    longest = result.shape.index(max(result.shape))
    spots = []
    for shift in (0, 1):
        where = [jax.random.randint(jax.random.fold_in(rng, axis), (), 0, length) for axis, length in enumerate(result.shape)]
        where[longest] = (where[longest] + shift) % result.shape[longest]
        spots.append(tuple(where))
    return result.at[spots[0]].set(least).at[spots[1]].set(largest)


def level_of(rng, extent, shards, least, top_value):
    def one(axis_at, parts):
        steps = jax.random.uniform(jax.random.fold_in(jax.random.fold_in(rng, 6), axis_at), (parts,), jnp.float32, least / len(shards), top_value / len(shards))
        return jnp.repeat(jnp.exp(steps), extent[axis_at] // parts).reshape((-1,) + (1,) * (len(extent) - axis_at - 1))

    gain = one(*shards[0])
    for cut in shards[1:]:
        gain = gain * one(*cut)
    return gain


def noise(key, dims, width, most, shards=(), kind=jnp.bfloat16):
    entries = jax.random.normal(key, dims, jnp.float32) * width
    if len(shards) > 0:
        entries = level_of(key, dims, shards, -0.22, 0.18) * entries
    return jnp.clip(entries, min=-most, max=most).astype(kind)


def setup_inputs(seed: int = 0) -> dict:
    arg_keys = jax.random.split(jax.random.key(seed), 8)
    return {
        "pattern_index": jax.random.randint(arg_keys[0], (GROUPS,), 0, NTABLE).astype(jnp.int32),
        "patterns": noise(arg_keys[1], (NTABLE, NX, NY), 1.0, 6.0, ((1, 64),), jnp.float32),
        "freq_bins": touch_ends(jax.random.randint(arg_keys[2], (K,), 0, NX), jax.random.fold_in(arg_keys[2], 1), 0, NX - 1).astype(jnp.int32),
        "absorption": jnp.clip(jnp.exp(math.log(0.5) - 2.3025851 * jax.random.uniform(arg_keys[3], (NX, NY, NZ), jnp.float32) ** level_of(arg_keys[3], (NX, NY, NZ), ((0, 64),), -0.2, 0.2)), 0.05, 0.5),
        "forward_start": noise(arg_keys[4], (GROUPS, NX, NY, NZ), 1.0, 6.0, ((0, 2), (1, 64)), jnp.float32),
        "adjoint_start": noise(arg_keys[5], (GROUPS, NX, NY, NZ), 1.0, 6.0, ((0, 2), (1, 64)), jnp.float32),
        "measured": noise(arg_keys[6], (GROUPS, 2, K, NY), 1.0, 6.0, ((0, 2), (3, 64)), jnp.float32),
    }


def sweep_weight(sweep):
    return 1.0 / (1.25 + 0.75 * math.cos(math.pi * (2 * sweep + 1) / (2 * SWEEPS)))

def relaxation(start, source, diag):
    field = start
    for sweep in range(SWEEPS):
        padded = jnp.pad(field, 1)
        beside_all = padded[2:, 1:-1, 1:-1] + padded[:-2, 1:-1, 1:-1]
        beside_all = beside_all + padded[1:-1, 2:, 1:-1] + padded[1:-1, :-2, 1:-1]
        beside_all = beside_all + padded[1:-1, 1:-1, 2:] + padded[1:-1, 1:-1, :-2]
        drive = -(diag * field - beside_all)
        drive = drive.at[:, :, 0].add(source)
        field = field + sweep_weight(sweep) * drive / diag
    return field

def reference(pattern_index, patterns, freq_bins, absorption, forward_start, adjoint_start, measured):
    diag = 6.0 + absorption
    positions = jnp.arange(NX, dtype=jnp.int32)
    phase = freq_bins[:, None] * positions[None, :] % NX
    angle = 2.0 * math.pi / NX * phase.astype(jnp.float32)
    cos_table = jnp.cos(angle) / math.sqrt(NX)
    sin_table = jnp.sin(angle) / math.sqrt(NX)
    high = lax.Precision.HIGHEST

    def one_group(total, inputs):
        index, start_fwd, start_adj, data = inputs
        source = patterns[index]
        fluence = relaxation(start_fwd, source, diag)
        surface = fluence[:, :, 0]
        real_part = jnp.dot(cos_table, surface, precision=high, preferred_element_type=jnp.float32)
        imag_part = -jnp.dot(sin_table, surface, precision=high, preferred_element_type=jnp.float32)
        model = jnp.stack([real_part, imag_part])
        misfit = model - data
        adjoint_source = jnp.dot(cos_table.T, misfit[0], precision=high, preferred_element_type=jnp.float32) - jnp.dot(sin_table.T, misfit[1], precision=high, preferred_element_type=jnp.float32)
        adjoint = relaxation(start_adj, adjoint_source, diag)
        return (total - fluence * adjoint, model)
    initial = jnp.zeros((NX, NY, NZ), jnp.float32)
    gradient, model = lax.scan(one_group, initial, (pattern_index, forward_start, adjoint_start, measured))
    return (gradient, model)
```

```python
import functools
import math

import jax
import jax.numpy as jnp
from jax import lax
from jax.experimental import pallas as pl
from jax.experimental.pallas import tpu as pltpu
from jax.sharding import Mesh
from jax.sharding import PartitionSpec as P

SWEEPS = 4
GX = ("gx_0", "gx_1", "gx_2", "gx_3")
ALL = ("pat",) + GX
CHUNKS = ((True, 0, 256), (True, 256, 256), (False, 0, 512))
HIGH = lax.Precision.HIGHEST
F32 = jnp.float32


def sweep_weight(sweep):
    return 1.0 / (1.25 + 0.75 * math.cos(math.pi * (2 * sweep + 1) / (2 * SWEEPS)))


def halo_rows(rows, ny):
    return rows + 8 if 2 * rows == ny else rows + 16


def chunk_start(meta_ref, sends, offset, half):
    pat = meta_ref[0]
    which = 1 - pat if sends else pat
    return which * half + offset


def iota(shape, dim):
    return lax.broadcasted_iota(jnp.int32, shape, dim)


def face_copies(meta, bufs, base, near, far, sem, chunk, ny):
    sends, offset, rows = chunk
    nh = halo_rows(rows, ny)
    y0 = chunk_start(meta, sends, offset, ny // 2)
    s = pl.multiple_of(jnp.clip(y0 - 8, 0, ny - nh) - base, 8)
    core = meta[4]
    outs = []
    for k, (arr, at, count) in enumerate(zip(bufs, (0, 4, 8), (4, 4, 3))):
        top = 8 - count
        for i, (dst, x) in enumerate(((far, core * top), (near, (1 - core) * top))):
            cp = pltpu.make_async_copy(
                arr.at[pl.ds(x, count), pl.ds(s, nh), :], dst.at[pl.ds(at, count)], sem.at[i, k]
            )
            cp.start()
            outs.append(cp)
    return outs


def faces_kernel(meta, fwd, adj, absn, near, far, fs, ad, ab, in_sem, sem, *, chunk, ny):
    sends, offset, rows = chunk
    nh = halo_rows(rows, ny)
    y0 = chunk_start(meta, sends, offset, ny // 2)
    s = pl.multiple_of(jnp.clip(y0 - 8, 0, ny - nh), 8)
    loads = []
    for i, (h, v) in enumerate(((fwd, fs), (adj, ad), (absn, ab))):
        cp = pltpu.make_async_copy(h.at[:, pl.ds(s, nh), :], v, in_sem.at[i])
        cp.start()
        loads.append(cp)
    for cp in loads:
        cp.wait()
    for cp in face_copies(meta, (fs, ad, ab), s, near, far, sem, chunk, ny):
        cp.wait()


def faces_call(meta, fwd, adj, absn, chunk):
    ny = fwd.shape[1]
    nh = halo_rows(chunk[2], ny)
    any_spec = pl.BlockSpec(memory_space=pl.ANY)
    return pl.pallas_call(
        functools.partial(faces_kernel, chunk=chunk, ny=ny),
        out_shape=[jax.ShapeDtypeStruct((11, nh, 128), F32)] * 2,
        in_specs=[pl.BlockSpec(memory_space=pltpu.SMEM)] + [any_spec] * 3,
        out_specs=[any_spec] * 2,
        scratch_shapes=[pltpu.VMEM((8, nh, 128), F32)] * 3
        + [pltpu.SemaphoreType.DMA((3,)), pltpu.SemaphoreType.DMA((2, 3))],
        name="faces",
    )(meta, fwd, adj, absn)


def pack_kernel(meta, fwd, adj, absn, pats, *rest, chunks, ny):
    n = 2 * len(chunks)
    faces = rest[:n]
    t1, t2, src, near, far, fs, ad, ab, p1, p2, in_sem, src_sem, face_sem = rest[n:]
    loads = []
    for i, (h, v) in enumerate(((fwd, fs), (adj, ad), (absn, ab))):
        cp = pltpu.make_async_copy(h, v, in_sem.at[i])
        cp.start()
        loads.append(cp)
    src_cp = pltpu.make_async_copy(pats.at[meta[3]], src, src_sem)
    src_cp.start()
    lane = iota((8, 128), 1)
    un = 8

    def pack(parts, dst):
        def body(t, carry):
            done = []
            for u in range(un):
                y = pl.multiple_of((t * un + u) * 8, 8)
                acc = jnp.zeros((8, 128), F32)
                for arr, base in parts:
                    for x in range(8):
                        at = base + 8 * x
                        v = arr[x, pl.ds(y, 8), :]
                        v = pltpu.roll(v, at, axis=1) if at else v
                        acc = jnp.where((lane >= at) & (lane < at + 8), v, acc)
                done.append((y, acc))
            for y, acc in done:
                dst[pl.ds(y, 8), :] = acc
            return carry

        lax.fori_loop(0, ny // (8 * un), body, 0)

    for cp in loads:
        cp.wait()
    outs = []
    for c, chunk in enumerate(chunks):
        outs += face_copies(
            meta, (fs, ad, ab), 0, faces[2 * c], faces[2 * c + 1], face_sem.at[c], chunk, ny
        )
    pack(((fs, 0), (ad, 64)), p1)
    pack(((ab, 0),), p2)
    for v in range(ny // 128):
        t1[:, v * 128 : (v + 1) * 128] = p1[v * 128 : (v + 1) * 128, :].T
        t2[:, v * 128 : (v + 1) * 128] = p2[v * 128 : (v + 1) * 128, :].T[:64]
    src_cp.wait()

    def high_face(dst):
        dst[0:32, :] = t1[32:64, :]
        dst[32:64, :] = t1[96:128, :]
        dst[64:88, :] = t2[40:64, :]
        dst[88:96, :] = pltpu.roll(src[...], 3, axis=0)

    def low_face(dst):
        dst[0:32, :] = t1[0:32, :]
        dst[32:64, :] = t1[64:96, :]
        dst[64:88, :] = t2[0:24, :]
        dst[88:96, :] = src[...]

    @pl.when(meta[4] == 0)
    def _():
        high_face(near)
        low_face(far)

    @pl.when(meta[4] != 0)
    def _():
        low_face(near)
        high_face(far)

    for cp in outs:
        cp.wait()


def pack_call(meta, fwd, adj, absn, pats, chunks):
    ny = fwd.shape[1]
    small = [(128, ny), (64, ny), (8, ny), (96, ny), (96, ny)]
    shapes = []
    for _, _, rows in chunks:
        shapes += [(11, halo_rows(rows, ny), 128)] * 2
    any_spec = pl.BlockSpec(memory_space=pl.ANY)
    vmem = pl.BlockSpec(memory_space=pltpu.VMEM)
    return pl.pallas_call(
        functools.partial(pack_kernel, chunks=chunks, ny=ny),
        out_shape=[jax.ShapeDtypeStruct(s, F32) for s in shapes + small],
        in_specs=[pl.BlockSpec(memory_space=pltpu.SMEM)] + [any_spec] * 4,
        out_specs=[any_spec] * len(shapes) + [vmem] * 5,
        scratch_shapes=[pltpu.VMEM((8, ny, 128), F32)] * 3
        + [pltpu.VMEM((ny, 128), F32)] * 2
        + [
            pltpu.SemaphoreType.DMA((3,)),
            pltpu.SemaphoreType.DMA(()),
            pltpu.SemaphoreType.DMA((len(chunks), 2, 3)),
        ],
        name="pack",
    )(meta, fwd, adj, absn, pats)


def group_transpose(v):
    row = iota((8, 128), 0)
    group = iota((8, 128), 1) // 16
    for b in (1, 2, 4):
        rb = (row // b) % 2
        gb = (group // b) % 2
        down = pltpu.roll(pltpu.roll(v, b, axis=0), 128 - 16 * b, axis=1)
        upw = pltpu.roll(pltpu.roll(v, 8 - b, axis=0), 16 * b, axis=1)
        v = jnp.where(rb == gb, v, jnp.where(rb == 1, down, upw))
    return v


def shallow_solve(meta, start, at, near, far, near_at, t2, f0, f1, r, s, ny):
    lo_ok = jnp.where(meta[1] > 0, 1.0, 0.0).astype(F32)
    hi_ok = jnp.where(meta[2] > 0, 1.0, 0.0).astype(F32)
    core0 = meta[4] == 0

    def side(row):
        a = near[row : row + 8, :]
        b = far[row : row + 8, :]
        return jnp.where(core0, b, a), jnp.where(core0, a, b)

    for i in range(4):
        f0[i], f0[12 + i] = side(near_at + 8 * i)
    for i in range(8):
        f0[4 + i] = start[at + 8 * i : at + 8 * i + 8, :]
        r[4 + i] = 1.0 / (6.0 + t2[8 * i : 8 * i + 8, :])
    for i in range(3):
        lo, hi = side(64 + 8 * i)
        r[1 + i] = lo_ok / (6.0 + lo)
        r[12 + i] = hi_ok / (6.0 + hi)
    zi = iota((8, ny), 0)
    yi = iota((8, ny), 1)
    bufs = (f0, f1)
    for k in range(SWEEPS):
        w = sweep_weight(k)
        old, new = bufs[k % 2], bufs[1 - k % 2]

        def pair(q, carry, old=old, new=new, w=w, k=k):
            p = k + 1 + 2 * q
            v = [old[p - 1 + i] for i in range(4)]
            for i in range(2):
                c = v[i + 1]
                nb = v[i] + v[i + 2]
                nb = nb + jnp.where(yi == 0, 0.0, pltpu.roll(c, 1, axis=1))
                nb = nb + jnp.where(yi == ny - 1, 0.0, pltpu.roll(c, ny - 1, axis=1))
                nb = nb + jnp.where(zi == 0, 0.0, pltpu.roll(c, 1, axis=0))
                nb = nb + jnp.where(zi == 7, 0.0, pltpu.roll(c, 7, axis=0))
                new[p + i] = (1.0 - w) * c + (w * r[p + i]) * (nb + s[p + i])
            return carry

        lax.fori_loop(0, 7 - k, pair, 0)


def forward_kernel(meta, t1, t2, src, near, far, fsh, surf, f0, f1, r, s, *, ny):
    z0 = iota((8, ny), 0) == 0
    core0 = meta[4] == 0
    for i in range(3):
        a = near[88 + i : 89 + i, :]
        b = far[88 + i : 89 + i, :]
        s[1 + i] = jnp.where(z0, jnp.where(core0, b, a), 0.0)
        s[12 + i] = jnp.where(z0, jnp.where(core0, a, b), 0.0)
    for i in range(8):
        s[4 + i] = jnp.where(z0, src[i : i + 1, :], 0.0)
    shallow_solve(meta, t1, 0, near, far, 0, t2, f0, f1, r, s, ny)
    for i in range(8):
        fsh[i] = f0[4 + i]
    top = jnp.concatenate([f0[4 + i, 0:1, :] for i in range(8)], axis=0)
    for v in range(ny // 128):
        surf[8 * v : 8 * v + 8, :] = group_transpose(top[:, 128 * v : 128 * v + 128])


def shallow_scratch(ny):
    return [pltpu.VMEM((16, 8, ny), F32)] * 4


def vmem_call(kernel, out_shapes, scratch, n_in):
    vmem = pl.BlockSpec(memory_space=pltpu.VMEM)
    return pl.pallas_call(
        kernel,
        out_shape=[jax.ShapeDtypeStruct(s, F32) for s in out_shapes],
        in_specs=[pl.BlockSpec(memory_space=pltpu.SMEM)] + [vmem] * n_in,
        out_specs=[vmem] * len(out_shapes),
        scratch_shapes=scratch,
    )


def adjoint_kernel(
    meta, t1, t2, got, near, far, fsh, send, keep, f0, f1, r, s, prod, *, ny
):
    z0 = iota((8, ny), 0) == 0
    for h in range(2):
        parts = []
        for v in range(ny // 128):
            parts.append(group_transpose(got[8 * v : 8 * v + 8, 128 * h : 128 * h + 128]))
        rows = jnp.concatenate(parts, axis=1)
        for j in range(8):
            s[8 * h + j] = jnp.where(z0, rows[j : j + 1, :], 0.0)
    shallow_solve(meta, t1, 64, near, far, 32, t2, f0, f1, r, s, ny)
    for i in range(8):
        prod[8 * i : 8 * i + 8, :] = -(fsh[i] * f0[4 + i])
    half = ny // 2

    @pl.when(meta[0] == 0)
    def _():
        keep[...] = prod[:, :half]
        send[...] = prod[:, half:]

    @pl.when(meta[0] != 0)
    def _():
        keep[...] = prod[:, half:]
        send[...] = prod[:, :half]


def data_kernel(meta, got, table, back, measured, model, send):
    lane_group = iota((32, 128), 1) // 16
    full = jnp.dot(table[...], got[...], precision=HIGH, preferred_element_type=F32)
    acc = jnp.zeros((32, 128), F32)
    for x in range(8):
        acc = acc + jnp.where(lane_group == x, full[32 * x : 32 * x + 32, :], 0.0)
    for shift in (64, 32, 16):
        acc = acc + pltpu.roll(acc, shift, axis=1)
    model[...] = acc
    misfit = acc - measured[...]
    rows = lax.dot_general(
        back[...], misfit, (((0,), (0,)), ((), ())), precision=HIGH, preferred_element_type=F32
    )
    count = rows.shape[0] // 16
    group = iota((count, 128), 1) // 16
    for h in range(2):
        out = jnp.zeros((count, 128), F32)
        for j in range(8):
            at = (8 * h + j) * count
            out = jnp.where(group == j, rows[at : at + count, :], out)
        send[:, 128 * h : 128 * h + 128] = out


def tile_count(tiles, most=66):
    return max(u for u in range(1, most + 1) if tiles % u == 0)


def deep_kernel(
    meta, fwd, adj, absn, near, far, out, f0, f1, a0, a1, rb, sem, *, sends, offset, rows, ny
):
    nh = halo_rows(rows, ny)
    y0 = chunk_start(meta, sends, offset, ny // 2)
    s = pl.multiple_of(jnp.clip(y0 - 8, 0, ny - nh), 8)
    off = pl.multiple_of(s - y0 + 16, 8)
    core = meta[4]

    def group(arr, at, count, buf, k):
        below = 4 - count
        cps = [
            pltpu.make_async_copy(
                arr.at[:, pl.ds(s, nh), :], buf.at[pl.ds(4, 8), pl.ds(off, nh), :], sem.at[k, 0]
            ),
            pltpu.make_async_copy(
                near.at[pl.ds(at, count)],
                buf.at[pl.ds(jnp.where(core == 0, 12, below), count), pl.ds(off, nh), :],
                sem.at[k, 1],
            ),
            pltpu.make_async_copy(
                far.at[pl.ds(at, count)],
                buf.at[pl.ds(jnp.where(core == 0, below, 12), count), pl.ds(off, nh), :],
                sem.at[k, 2],
            ),
        ]
        for cp in cps:
            cp.start()
        return cps

    r_cps = group(absn, 8, 3, rb, 0)
    f_cps = group(fwd, 0, 4, f0, 1)
    a_cps = group(adj, 4, 4, a0, 2)
    zero = jnp.zeros((16, 8, 128), F32)

    def edges(buf):
        @pl.when(y0 == 0)
        def _():
            buf[:, 8:16, :] = zero

        @pl.when(y0 + rows == ny)
        def _():
            buf[:, rows + 16 : rows + 24, :] = zero

    edges(f0)
    edges(a0)
    tiles = (rows + 16) // 8
    for cp in r_cps:
        cp.wait()

    def invert(p, carry):
        ok = jnp.where(p < 4, meta[1], jnp.where(p >= 12, meta[2], 1))
        ok = jnp.where(ok > 0, 1.0, 0.0).astype(F32)
        un = tile_count(tiles)

        def block(t, c):
            ys = [pl.multiple_of(8 + (t * un + u) * 8, 8) for u in range(un)]
            new = [ok / (6.0 + rb[p, pl.ds(y, 8), :]) for y in ys]
            for y, v in zip(ys, new):
                rb[p, pl.ds(y, 8), :] = v
            return c

        return lax.fori_loop(0, tiles // un, block, carry)

    lax.fori_loop(1, 15, invert, 0)
    edges(rb)
    last = iota((8, 128), 1) == 127

    def sweep(buf, k, begin, count, store):
        w = sweep_weight(k)
        un = tile_count(count)

        def pair(q, carry):
            p = k + 1 + 2 * q

            def block(t, cc):
                for u in range(un):
                    y = pl.multiple_of(begin + (t * un + u) * 8, 8)
                    v = [buf[p - 1 + i, pl.ds(y, 8), :] for i in range(4)]
                    for i in range(2):
                        c = v[i + 1]
                        ym = buf[p + i, pl.ds(y - 1, 8), :]
                        yp = buf[p + i, pl.ds(y + 1, 8), :]
                        zl = pltpu.roll(c, 1, axis=1)
                        zr = jnp.where(last, 0.0, pltpu.roll(c, 127, axis=1))
                        nb = ((v[i] + v[i + 2]) + (ym + yp)) + (zl + zr)
                        new = ((1.0 - w) / w) * c + rb[p + i, pl.ds(y, 8), :] * nb
                        store(p + i, y, new)
                return cc

            return lax.fori_loop(0, count // un, block, carry)

        lax.fori_loop(0, 7 - k, pair, 0)

    def into(buf):
        def store(p, y, new):
            buf[p, pl.ds(y, 8), :] = new

        return store

    scale = -math.prod(sweep_weight(k) for k in range(SWEEPS)) ** 2

    def product(p, y, new):
        at = pl.multiple_of(y - 16, 8)
        out[p - 4, pl.ds(at, 8), :] = (scale * f0[p, pl.ds(y, 8), :]) * new

    for bufs, cps in (((f0, f1), f_cps), ((a0, a1), a_cps)):
        for cp in cps:
            cp.wait()
        for k in range(SWEEPS):
            src, dst = bufs[k % 2], bufs[1 - k % 2]
            if k < SWEEPS - 1:
                sweep(src, k, 8, tiles, into(dst))
            elif src is f1:
                sweep(src, k, 16, rows // 8, into(dst))
            else:
                sweep(src, k, 16, rows // 8, product)


def deep_call(meta, fwd, adj, absn, near, far, chunk):
    sends, offset, rows = chunk
    ny = fwd.shape[1]
    any_spec = pl.BlockSpec(memory_space=pl.ANY)
    return pl.pallas_call(
        functools.partial(deep_kernel, sends=sends, offset=offset, rows=rows, ny=ny),
        out_shape=jax.ShapeDtypeStruct((8, rows, 128), F32),
        in_specs=[pl.BlockSpec(memory_space=pltpu.SMEM)] + [any_spec] * 5,
        out_specs=pl.BlockSpec(memory_space=pltpu.VMEM),
        scratch_shapes=[
            pltpu.VMEM((16, rows + 32, 128), F32),
            pltpu.VMEM((16, rows + 32, 128), F32),
            pltpu.VMEM((16, rows + 32, 128), F32),
            pltpu.VMEM((16, rows + 32, 128), F32),
            pltpu.VMEM((16, rows + 32, 128), F32),
            pltpu.SemaphoreType.DMA((3, 3)),
        ],
    )(meta, fwd, adj, absn, near, far)


def final_kernel(*refs, n_own, n_got):
    own = refs[:n_own]
    got = refs[n_own : n_own + n_got]
    keep, recv, out, packed = refs[n_own + n_got :]
    x = pl.program_id(0)

    @pl.when(x == 0)
    def _():
        both = keep[...] + recv[...]
        for v in range(both.shape[1] // 128):
            cols = both[:, 128 * v : 128 * v + 128]
            cols = jnp.concatenate([cols, cols], axis=0)
            packed[128 * v : 128 * v + 128, :] = cols.T

    def cover(parts):
        at = 0
        found = []
        for ref in parts:
            found.append((at, ref.shape[1], ref))
            at += ref.shape[1]
        return found

    cuts = sorted({a for a, _, _ in cover(own)} | {a for a, _, _ in cover(got)} | {out.shape[1]})

    def piece(parts, a, b):
        for at, size, ref in cover(parts):
            if at <= a and b <= at + size:
                return ref[0, a - at : b - at, :]

    for a, b in zip(cuts[:-1], cuts[1:]):
        shallow = pltpu.roll(packed[a:b, :], (128 - 8 * x) % 128, axis=1)
        deep = piece(own, a, b) + piece(got, a, b)
        out[0, a:b, :] = jnp.where(iota((b - a, 128), 1) < 4, shallow, deep)


def final_call(own, got, keep, recv):
    half = keep.shape[1]

    def spec(a):
        return pl.BlockSpec((1, a.shape[1], 128), lambda x: (x, 0, 0))

    whole = pl.BlockSpec((64, half), lambda x: (0, 0))
    return pl.pallas_call(
        functools.partial(final_kernel, n_own=len(own), n_got=len(got)),
        out_shape=jax.ShapeDtypeStruct((8, half, 128), F32),
        grid=(8,),
        in_specs=[spec(a) for a in own + got] + [whole, whole],
        out_specs=pl.BlockSpec((1, half, 128), lambda x: (x, 0, 0)),
        scratch_shapes=[pltpu.VMEM((half, 128), F32)],
        name="final",
    )(*own, *got, keep, recv)


def after(value, *others):
    return lax.optimization_barrier((value, others))[0]


def shards(pattern_index, patterns, freq_bins, absorption, forward_start, adjoint_start, measured):
    ny = forward_start.shape[2]
    parts = lax.axis_size(GX)
    total_x = parts * 8
    fwd = forward_start[0]
    adj = adjoint_start[0]
    gx = lax.axis_index(GX)
    meta = jnp.stack(
        [
            lax.axis_index("pat"),
            (gx > 0).astype(jnp.int32),
            (gx < parts - 1).astype(jnp.int32),
            pattern_index[0],
            gx % 2,
        ]
    ).astype(jnp.int32)

    lid = [[p * parts + g for g in range(parts)] for p in range(2)]
    near_pairs = [(r[g], r[g ^ 1]) for r in lid for g in range(parts)]
    far_pairs = []
    for r in lid:
        for g in range(1, parts - 1, 2):
            far_pairs += [(r[g], r[g + 1]), (r[g + 1], r[g])]
    pat_pairs = [(lid[p][g], lid[1 - p][g]) for p in range(2) for g in range(parts)]

    def exchange(near, far):
        near = lax.ppermute(near, ALL, near_pairs)
        far = lax.ppermute(far, ALL, far_pairs)
        return near, far

    out = faces_call(meta, fwd, adj, absorption, CHUNKS[0])
    halos = [exchange(*out)]
    meta = after(meta, *out)
    out = pack_call(meta, fwd, adj, absorption, patterns, CHUNKS[1:])
    t1, t2, src, near, far = out[-5:]
    meta = after(meta, near, far)
    near, far = exchange(near, far)
    for c in range(1, len(CHUNKS)):
        halos.append(exchange(*out[2 * c - 2 : 2 * c]))

    def table(phase):
        angle = 2.0 * math.pi / total_x * (phase % total_x).astype(F32)
        scale = math.sqrt(total_x)
        return jnp.cos(angle) / scale, -(jnp.sin(angle) / scale)

    bins = after(freq_bins, meta)
    x_at = jnp.arange(parts, dtype=jnp.int32) * 8
    x_in = jnp.arange(8, dtype=jnp.int32)[:, None] + x_at[None, :]
    x_out = (jnp.arange(-4, 12, dtype=jnp.int32)[:, None] + x_at[None, :]).reshape(-1)
    to_data = jnp.concatenate(table(bins[None, :, None] * x_in[:, None, :]), axis=1)
    to_data = to_data.reshape(8 * 32, parts)
    from_data = jnp.concatenate(table(bins[:, None] * x_out[None, :]), axis=0)
    seen = jnp.tile(after(measured, meta).reshape(32, 16), (1, 8))
    meta = after(meta, to_data, from_data, seen)

    own, arrived = [], []

    def deep(meta, c):
        terms = deep_call(meta, fwd, adj, absorption, *halos[c], CHUNKS[c])
        if CHUNKS[c][0]:
            arrived.append(lax.ppermute(terms, ALL, pat_pairs))
        else:
            own.append(terms)
        return after(meta, terms)

    meta = deep(meta, 0)
    fsh, surf = vmem_call(
        functools.partial(forward_kernel, ny=ny), [(8, 8, ny), (parts, 128)], shallow_scratch(ny), 5
    )(meta, t1, t2, src, near, far)
    meta = after(meta, surf)
    got = lax.all_to_all(surf, GX, 0, 0, tiled=True)
    meta = deep(meta, 1)
    model, rows = vmem_call(data_kernel, [(32, 128), (parts, 256)], [], 4)(
        meta, got, to_data, from_data, seen
    )
    meta = after(meta, rows)
    back = lax.all_to_all(rows, GX, 0, 0, tiled=True)
    for c in range(2, len(CHUNKS)):
        meta = deep(meta, c)
    send, keep = vmem_call(
        functools.partial(adjoint_kernel, ny=ny),
        [(64, ny // 2), (64, ny // 2)],
        shallow_scratch(ny) + [pltpu.VMEM((64, ny), F32)],
        6,
    )(meta, t1, t2, back, near, far, fsh)
    recv = lax.ppermute(send, ALL, pat_pairs)
    gradient = final_call(own, arrived, keep, recv)
    return (gradient, model[:, :16].reshape(1, 2, 16, 16))


def solution(mesh):
    torus = Mesh(mesh.devices.reshape(mesh.shape["pat"], 4, 2, 4, 2), ALL)
    in_specs = (
        P("pat"),
        P(None, GX, None),
        P(),
        P(GX, None, None),
        P("pat", GX, None, None),
        P("pat", GX, None, None),
        P("pat", None, None, GX),
    )
    out_specs = (P(GX, "pat", None), P("pat", None, None, GX))

    return jax.shard_map(
        shards, mesh=torus, in_specs=in_specs, out_specs=out_specs, check_vma=False
    )
```

```python
import functools
import math

import jax
import jax.numpy as jnp
from jax import lax
from jax.experimental import pallas as pl
from jax.experimental.pallas import tpu as pltpu
from jax.sharding import Mesh
from jax.sharding import PartitionSpec as P

SWEEPS = 4
GX = ("gx_0", "gx_1", "gx_2", "gx_3")
ALL = ("pat",) + GX
CHUNKS = ((True, 0, 256), (True, 256, 256), (False, 0, 512))
HIGH = lax.Precision.HIGHEST
F32 = jnp.float32
BF16 = jnp.bfloat16
MXU_PLANES = (1,)
PLANES = 2


def sweep_weight(sweep):
    return 1.0 / (1.25 + 0.75 * math.cos(math.pi * (2 * sweep + 1) / (2 * SWEEPS)))


def halo_rows(rows, ny):
    return rows + 8 if 2 * rows == ny else rows + 16


def chunk_start(meta_ref, sends, offset, half):
    pat = meta_ref[0]
    which = 1 - pat if sends else pat
    return which * half + offset


def iota(shape, dim):
    return lax.broadcasted_iota(jnp.int32, shape, dim)


def face_copies(meta, bufs, base, near, far, sem, chunk, ny):
    sends, offset, rows = chunk
    nh = halo_rows(rows, ny)
    y0 = chunk_start(meta, sends, offset, ny // 2)
    s = pl.multiple_of(jnp.clip(y0 - 8, 0, ny - nh) - base, 8)
    core = meta[4]
    outs = []
    for k, (arr, at, count) in enumerate(zip(bufs, (0, 4, 8), (4, 4, 3))):
        top = 8 - count
        for i, (dst, x) in enumerate(((far, core * top), (near, (1 - core) * top))):
            cp = pltpu.make_async_copy(
                arr.at[pl.ds(x, count), pl.ds(s, nh), :], dst.at[pl.ds(at, count)], sem.at[i, k]
            )
            cp.start()
            outs.append(cp)
    return outs


SHALLOW_ROWS = 96


def shallow_place(v, row, nh):
    at = SHALLOW_ROWS * v + row
    return at // nh, at % nh


def head_kernel(meta, fwd, adj, absn, pats, *rest, chunks, ny):
    n = 2 * len(chunks)
    faces = rest[:n]
    t1, t2, src, fs, ad, ab, near, far, in_sem, src_sem, face_sem, sh_sem = rest[n:]
    loads = []
    for i, (h, v) in enumerate(((fwd, fs), (adj, ad), (absn, ab))):
        cp = pltpu.make_async_copy(h, v, in_sem.at[i])
        cp.start()
        loads.append(cp)
    src_cp = pltpu.make_async_copy(pats.at[meta[3]], src, src_sem)
    src_cp.start()

    def pack(arr, dst, base):
        def body(x, carry):
            at = pl.multiple_of(base + 8 * x, 8)
            for v in range(ny // 128):
                dst[pl.ds(at, 8), 128 * v : 128 * v + 128] = arr[x, 128 * v : 128 * v + 128, :].T[:8]
            return carry

        lax.fori_loop(0, 8, body, 0)

    loads[0].wait()
    pack(fs, t1, 0)
    loads[1].wait()
    pack(ad, t1, 64)
    loads[2].wait()
    outs = []
    for c, chunk in enumerate(chunks):
        outs += face_copies(
            meta, (fs, ad, ab), 0, faces[2 * c], faces[2 * c + 1], face_sem.at[c], chunk, ny
        )
    pack(ab, t2, 0)
    src_cp.wait()
    nh = halo_rows(chunks[0][2], ny)

    def put(dst, value, row):
        for v in range(ny // 128):
            p, r = shallow_place(v, row, nh)
            dst[p, r : r + 8, :] = value[:, 128 * v : 128 * v + 128]

    def high_face(dst):
        for i in range(4):
            put(dst, t1[32 + 8 * i : 40 + 8 * i, :], 8 * i)
            put(dst, t1[96 + 8 * i : 104 + 8 * i, :], 32 + 8 * i)
        for i in range(3):
            put(dst, t2[40 + 8 * i : 48 + 8 * i, :], 64 + 8 * i)
        put(dst, pltpu.roll(src[...], 3, axis=0), 88)

    def low_face(dst):
        for i in range(4):
            put(dst, t1[8 * i : 8 * i + 8, :], 8 * i)
            put(dst, t1[64 + 8 * i : 72 + 8 * i, :], 32 + 8 * i)
        for i in range(3):
            put(dst, t2[8 * i : 8 * i + 8, :], 64 + 8 * i)
        put(dst, src[...], 88)

    @pl.when(meta[4] == 0)
    def _():
        high_face(near)
        low_face(far)

    @pl.when(meta[4] != 0)
    def _():
        low_face(near)
        high_face(far)

    for i, (v, h) in enumerate(((near, faces[0]), (far, faces[1]))):
        cp = pltpu.make_async_copy(v, h.at[pl.ds(11, 3)], sh_sem.at[i])
        cp.start()
        outs.append(cp)
    for cp in outs:
        cp.wait()


def head_call(meta, fwd, adj, absn, pats, chunks):
    ny = fwd.shape[1]
    small = [(128, ny), (64, ny), (8, ny)]
    shapes = []
    for c, (_, _, rows) in enumerate(chunks):
        shapes += [(11 if c else 14, halo_rows(rows, ny), 128)] * 2
    any_spec = pl.BlockSpec(memory_space=pl.ANY)
    vmem = pl.BlockSpec(memory_space=pltpu.VMEM)
    return pl.pallas_call(
        functools.partial(head_kernel, chunks=chunks, ny=ny),
        out_shape=[jax.ShapeDtypeStruct(s, F32) for s in shapes + small],
        in_specs=[pl.BlockSpec(memory_space=pltpu.SMEM)] + [any_spec] * 4,
        out_specs=[any_spec] * len(shapes) + [vmem] * 3,
        scratch_shapes=[pltpu.VMEM((8, ny, 128), F32)] * 3
        + [pltpu.VMEM((3, shapes[0][1], 128), F32)] * 2
        + [
            pltpu.SemaphoreType.DMA((3,)),
            pltpu.SemaphoreType.DMA(()),
            pltpu.SemaphoreType.DMA((len(chunks), 2, 3)),
            pltpu.SemaphoreType.DMA((2,)),
        ],
        name="head",
    )(meta, fwd, adj, absn, pats)


def group_transpose(v):
    row = iota((8, 128), 0)
    group = iota((8, 128), 1) // 16
    for b in (1, 2, 4):
        rb = (row // b) % 2
        gb = (group // b) % 2
        down = pltpu.roll(pltpu.roll(v, b, axis=0), 128 - 16 * b, axis=1)
        upw = pltpu.roll(pltpu.roll(v, 8 - b, axis=0), 16 * b, axis=1)
        v = jnp.where(rb == gb, v, jnp.where(rb == 1, down, upw))
    return v


def shallow_side(near, far, core0, row, ny):
    a, b = [], []
    for v in range(ny // 128):
        p, r = shallow_place(v, row, near.shape[1])
        a.append(near[p, r : r + 8, :])
        b.append(far[p, r : r + 8, :])
    a = jnp.concatenate(a, axis=1)
    b = jnp.concatenate(b, axis=1)
    return jnp.where(core0, b, a), jnp.where(core0, a, b)


def fetch_shallow(near_hbm, far_hbm, near, far, sem):
    cps = []
    for i, (h, v) in enumerate(((near_hbm, near), (far_hbm, far))):
        cp = pltpu.make_async_copy(h.at[pl.ds(11, 3)], v, sem.at[i])
        cp.start()
        cps.append(cp)
    for cp in cps:
        cp.wait()


def shallow_solve(meta, start, at, near, far, near_at, t2, f0, f1, r, s, ny):
    lo_ok = jnp.where(meta[1] > 0, 1.0, 0.0).astype(F32)
    hi_ok = jnp.where(meta[2] > 0, 1.0, 0.0).astype(F32)
    core0 = meta[4] == 0

    def side(row):
        return shallow_side(near, far, core0, row, ny)

    for i in range(4):
        f0[i], f0[12 + i] = side(near_at + 8 * i)
    for i in range(8):
        f0[4 + i] = start[at + 8 * i : at + 8 * i + 8, :]
        r[4 + i] = 1.0 / (6.0 + t2[8 * i : 8 * i + 8, :])
    for i in range(3):
        lo, hi = side(64 + 8 * i)
        r[1 + i] = lo_ok / (6.0 + lo)
        r[12 + i] = hi_ok / (6.0 + hi)
    zi = iota((8, ny), 0)
    yi = iota((8, ny), 1)
    bufs = (f0, f1)
    for k in range(SWEEPS):
        w = sweep_weight(k)
        old, new = bufs[k % 2], bufs[1 - k % 2]

        def pair(q, carry, old=old, new=new, w=w, k=k):
            p = k + 1 + 2 * q
            v = [old[p - 1 + i] for i in range(4)]
            for i in range(2):
                c = v[i + 1]
                nb = v[i] + v[i + 2]
                nb = nb + jnp.where(yi == 0, 0.0, pltpu.roll(c, 1, axis=1))
                nb = nb + jnp.where(yi == ny - 1, 0.0, pltpu.roll(c, ny - 1, axis=1))
                nb = nb + jnp.where(zi == 0, 0.0, pltpu.roll(c, 1, axis=0))
                nb = nb + jnp.where(zi == 7, 0.0, pltpu.roll(c, 7, axis=0))
                new[p + i] = (1.0 - w) * c + (w * r[p + i]) * (nb + s[p + i])
            return carry

        lax.fori_loop(0, 7 - k, pair, 0)


def forward_kernel(
    meta, t1, t2, src, near_hbm, far_hbm, fsh, surf, near, far, sem, f0, f1, r, s, *, ny
):
    fetch_shallow(near_hbm, far_hbm, near, far, sem)
    z0 = iota((8, ny), 0) == 0
    lo, hi = shallow_side(near, far, meta[4] == 0, 88, ny)
    for i in range(3):
        s[1 + i] = jnp.where(z0, lo[i : i + 1, :], 0.0)
        s[12 + i] = jnp.where(z0, hi[i : i + 1, :], 0.0)
    for i in range(8):
        s[4 + i] = jnp.where(z0, src[i : i + 1, :], 0.0)
    shallow_solve(meta, t1, 0, near, far, 0, t2, f0, f1, r, s, ny)
    for i in range(8):
        fsh[i] = f0[4 + i]
    top = jnp.concatenate([f0[4 + i, 0:1, :] for i in range(8)], axis=0)
    for v in range(ny // 128):
        surf[8 * v : 8 * v + 8, :] = group_transpose(top[:, 128 * v : 128 * v + 128])


def shallow_scratch(ny, nh):
    return (
        [pltpu.VMEM((3, nh, 128), F32)] * 2
        + [pltpu.SemaphoreType.DMA((2,))]
        + [pltpu.VMEM((16, 8, ny), F32)] * 4
    )


def vmem_call(kernel, out_shapes, scratch, n_in, n_any=0):
    vmem = pl.BlockSpec(memory_space=pltpu.VMEM)
    any_spec = pl.BlockSpec(memory_space=pl.ANY)
    return pl.pallas_call(
        kernel,
        out_shape=[jax.ShapeDtypeStruct(s, F32) for s in out_shapes],
        in_specs=[pl.BlockSpec(memory_space=pltpu.SMEM)] + [vmem] * n_in + [any_spec] * n_any,
        out_specs=[vmem] * len(out_shapes),
        scratch_shapes=scratch,
    )


def adjoint_kernel(
    meta, t1, t2, got, fsh, near_hbm, far_hbm, send, keep, near, far, sem, f0, f1, r, s, prod, *, ny
):
    fetch_shallow(near_hbm, far_hbm, near, far, sem)
    z0 = iota((8, ny), 0) == 0
    for h in range(2):
        parts = []
        for v in range(ny // 128):
            parts.append(group_transpose(got[8 * v : 8 * v + 8, 128 * h : 128 * h + 128]))
        rows = jnp.concatenate(parts, axis=1)
        for j in range(8):
            s[8 * h + j] = jnp.where(z0, rows[j : j + 1, :], 0.0)
    shallow_solve(meta, t1, 64, near, far, 32, t2, f0, f1, r, s, ny)
    for i in range(8):
        prod[8 * i : 8 * i + 8, :] = -(fsh[i] * f0[4 + i])
    half = ny // 2

    @pl.when(meta[0] == 0)
    def _():
        keep[...] = prod[:, :half]
        send[...] = prod[:, half:]

    @pl.when(meta[0] != 0)
    def _():
        keep[...] = prod[:, half:]
        send[...] = prod[:, :half]


def data_kernel(meta, got, table, back, measured, model, send, seen):
    lane_group = iota((32, 128), 1) // 16
    full = jnp.dot(table[...], got[...], precision=HIGH, preferred_element_type=F32)
    acc = jnp.zeros((32, 128), F32)
    for x in range(8):
        acc = acc + jnp.where(lane_group == x, full[32 * x : 32 * x + 32, :], 0.0)
    for shift in (64, 32, 16):
        acc = acc + pltpu.roll(acc, shift, axis=1)
    model[...] = acc
    seen[...] = jnp.zeros((32, 128), F32)
    seen[:, :16] = measured[...]
    data = seen[...]
    for shift in (16, 32, 64):
        data = data + pltpu.roll(data, shift, axis=1)
    misfit = acc - data
    rows = lax.dot_general(
        back[...], misfit, (((0,), (0,)), ((), ())), precision=HIGH, preferred_element_type=F32
    )
    count = rows.shape[0] // 16
    group = iota((count, 128), 1) // 16
    for h in range(2):
        out = jnp.zeros((count, 128), F32)
        for j in range(8):
            at = (8 * h + j) * count
            out = jnp.where(group == j, rows[at : at + count, :], out)
        send[:, 128 * h : 128 * h + 128] = out


def tile_count(tiles, most=66):
    return max(u for u in range(1, most + 1) if tiles % u == 0)


def deep_kernel(
    meta, fwd, adj, absn, near, far, out, f0, f1, a0, a1, rb, zb, sem, *, sends, offset, rows, ny
):
    nh = halo_rows(rows, ny)
    y0 = chunk_start(meta, sends, offset, ny // 2)
    s = pl.multiple_of(jnp.clip(y0 - 8, 0, ny - nh), 8)
    off = pl.multiple_of(s - y0 + 16, 8)
    core = meta[4]

    def group(arr, at, count, buf, k):
        below = 4 - count
        cps = [
            pltpu.make_async_copy(
                arr.at[:, pl.ds(s, nh), :], buf.at[pl.ds(4, 8), pl.ds(off, nh), :], sem.at[k, 0]
            ),
            pltpu.make_async_copy(
                near.at[pl.ds(at, count)],
                buf.at[pl.ds(jnp.where(core == 0, 12, below), count), pl.ds(off, nh), :],
                sem.at[k, 1],
            ),
            pltpu.make_async_copy(
                far.at[pl.ds(at, count)],
                buf.at[pl.ds(jnp.where(core == 0, below, 12), count), pl.ds(off, nh), :],
                sem.at[k, 2],
            ),
        ]
        for cp in cps:
            cp.start()
        return cps

    r_cps = group(absn, 8, 3, rb, 0)
    f_cps = group(fwd, 0, 4, f0, 1)
    a_cps = group(adj, 4, 4, a0, 2)
    zero = jnp.zeros((16, 8, 128), F32)

    def edges(buf):
        @pl.when(y0 == 0)
        def _():
            buf[:, 8:16, :] = zero

        @pl.when(y0 + rows == ny)
        def _():
            buf[:, rows + 16 : rows + 24, :] = zero

    edges(f0)
    edges(a0)
    tiles = (rows + 16) // 8
    for cp in r_cps:
        cp.wait()

    def invert(p, carry):
        ok = jnp.where(p < 4, meta[1], jnp.where(p >= 12, meta[2], 1))
        ok = jnp.where(ok > 0, 1.0, 0.0).astype(F32)
        un = tile_count(tiles)

        def block(t, c):
            ys = [pl.multiple_of(8 + (t * un + u) * 8, 8) for u in range(un)]
            new = [ok / (6.0 + rb[p, pl.ds(y, 8), :]) for y in ys]
            for y, v in zip(ys, new):
                rb[p, pl.ds(y, 8), :] = v
            return c

        return lax.fori_loop(0, tiles // un, block, carry)

    lax.fori_loop(1, 15, invert, 0)
    edges(rb)
    last = iota((8, 128), 1) == 127
    apart = jnp.abs(iota((128, 128), 0) - iota((128, 128), 1))
    shifts = jnp.where(apart == 1, 1.0, 0.0).astype(BF16)
    shifts = jnp.concatenate([shifts, shifts], axis=0)

    def sweep(buf, k, begin, count, store):
        w = sweep_weight(k)

        def pair(q, carry):
            p = k + 1 + 2 * q
            for i in MXU_PLANES:
                c = buf[p + i, begin : begin + 8 * count, :]
                head = c.astype(BF16)
                tail = (c - head.astype(F32)).astype(BF16)
                both = jnp.concatenate([head, tail], axis=1)
                zb[i, : 8 * count, :] = jnp.dot(both, shifts, preferred_element_type=F32)
            for t in range(count):
                y = begin + 8 * t
                v = [buf[p - 1 + i, y : y + 8, :] for i in range(4)]
                for i in range(2):
                    ym = buf[p + i, y - 1 : y + 7, :]
                    yp = buf[p + i, y + 1 : y + 9, :]
                    if i in MXU_PLANES:
                        zs = zb[i, 8 * t : 8 * t + 8, :]
                    else:
                        zr = jnp.where(last, 0.0, pltpu.roll(v[i + 1], 127, axis=1))
                        zs = pltpu.roll(v[i + 1], 1, axis=1) + zr
                    nb = ((v[i] + v[i + 2]) + (ym + yp)) + zs
                    store(p + i, y, ((1.0 - w) / w) * v[i + 1] + rb[p + i, y : y + 8, :] * nb)
            return carry

        lax.fori_loop(0, 7 - k, pair, 0)

    def into(buf):
        def store(p, y, new):
            buf[p, y : y + 8, :] = new

        return store

    scale = -math.prod(sweep_weight(k) for k in range(SWEEPS)) ** 2

    def product(p, y, new):
        out[p - 4, y - 16 : y - 8, :] = (scale * f0[p, y : y + 8, :]) * new

    for bufs, cps in (((f0, f1), f_cps), ((a0, a1), a_cps)):
        for cp in cps:
            cp.wait()
        for k in range(SWEEPS):
            src, dst = bufs[k % 2], bufs[1 - k % 2]
            if k < SWEEPS - 1:
                sweep(src, k, 8, tiles, into(dst))
            elif src is f1:
                sweep(src, k, 16, rows // 8, into(dst))
            else:
                sweep(src, k, 16, rows // 8, product)


def deep_call(meta, fwd, adj, absn, near, far, chunk):
    sends, offset, rows = chunk
    ny = fwd.shape[1]
    any_spec = pl.BlockSpec(memory_space=pl.ANY)
    return pl.pallas_call(
        functools.partial(deep_kernel, sends=sends, offset=offset, rows=rows, ny=ny),
        out_shape=jax.ShapeDtypeStruct((8, rows, 128), F32),
        in_specs=[pl.BlockSpec(memory_space=pltpu.SMEM)] + [any_spec] * 5,
        out_specs=pl.BlockSpec(memory_space=pltpu.VMEM),
        scratch_shapes=[
            pltpu.VMEM((16, rows + 32, 128), F32),
            pltpu.VMEM((16, rows + 32, 128), F32),
            pltpu.VMEM((16, rows + 32, 128), F32),
            pltpu.VMEM((16, rows + 32, 128), F32),
            pltpu.VMEM((16, rows + 32, 128), F32),
            pltpu.VMEM((2, rows + 16, 128), F32),
            pltpu.SemaphoreType.DMA((3, 3)),
        ],
    )(meta, fwd, adj, absn, near, far)


def final_kernel(*refs, n_own, n_got):
    own = refs[:n_own]
    got = refs[n_own : n_own + n_got]
    keep, recv, out, packed = refs[n_own + n_got :]
    x = pl.program_id(0)

    @pl.when(x == 0)
    def _():
        both = keep[...] + recv[...]
        for v in range(both.shape[1] // 128):
            cols = both[:, 128 * v : 128 * v + 128]
            cols = jnp.concatenate([cols, cols], axis=0)
            packed[128 * v : 128 * v + 128, :] = cols.T

    def cover(parts):
        at = 0
        found = []
        for ref in parts:
            found.append((at, ref.shape[1], ref))
            at += ref.shape[1]
        return found

    cuts = sorted({a for a, _, _ in cover(own)} | {a for a, _, _ in cover(got)} | {out.shape[1]})

    def piece(parts, a, b, i):
        for at, size, ref in cover(parts):
            if at <= a and b <= at + size:
                return ref[i, a - at : b - at, :]

    for a, b in zip(cuts[:-1], cuts[1:]):
        for i in range(PLANES):
            shift = (128 - 8 * (PLANES * x + i)) % 128
            shallow = pltpu.roll(packed[a:b, :], shift, axis=1)
            deep = piece(own, a, b, i) + piece(got, a, b, i)
            out[i, a:b, :] = jnp.where(iota((b - a, 128), 1) < 4, shallow, deep)


def final_call(own, got, keep, recv):
    half = keep.shape[1]

    def spec(a):
        return pl.BlockSpec((PLANES, a.shape[1], 128), lambda x: (x, 0, 0))

    whole = pl.BlockSpec((64, half), lambda x: (0, 0))
    return pl.pallas_call(
        functools.partial(final_kernel, n_own=len(own), n_got=len(got)),
        out_shape=jax.ShapeDtypeStruct((8, half, 128), F32),
        grid=(8 // PLANES,),
        in_specs=[spec(a) for a in own + got] + [whole, whole],
        out_specs=pl.BlockSpec((PLANES, half, 128), lambda x: (x, 0, 0)),
        scratch_shapes=[pltpu.VMEM((half, 128), F32)],
        name="final",
    )(*own, *got, keep, recv)


def after(value, *others):
    return lax.optimization_barrier((value, others))[0]


def shards(pattern_index, patterns, freq_bins, absorption, forward_start, adjoint_start, measured):
    ny = forward_start.shape[2]
    parts = lax.axis_size(GX)
    total_x = parts * 8
    fwd = forward_start[0]
    adj = adjoint_start[0]
    gx = lax.axis_index(GX)
    meta = jnp.stack(
        [
            lax.axis_index("pat"),
            (gx > 0).astype(jnp.int32),
            (gx < parts - 1).astype(jnp.int32),
            pattern_index[0],
            gx % 2,
        ]
    ).astype(jnp.int32)

    lid = [[p * parts + g for g in range(parts)] for p in range(2)]
    near_pairs = [(r[g], r[g ^ 1]) for r in lid for g in range(parts)]
    far_pairs = []
    for r in lid:
        for g in range(1, parts - 1, 2):
            far_pairs += [(r[g], r[g + 1]), (r[g + 1], r[g])]
    pat_pairs = [(lid[p][g], lid[1 - p][g]) for p in range(2) for g in range(parts)]

    def exchange(near, far):
        near = lax.ppermute(near, ALL, near_pairs)
        far = lax.ppermute(far, ALL, far_pairs)
        return near, far

    out = head_call(meta, fwd, adj, absorption, patterns, CHUNKS)
    t1, t2, src = out[-3:]
    halos = [exchange(out[2 * c], out[2 * c + 1]) for c in range(len(CHUNKS))]
    near, far = halos[0]
    meta = after(meta, t1)

    def table(phase):
        angle = 2.0 * math.pi / total_x * (phase % total_x).astype(F32)
        scale = math.sqrt(total_x)
        return jnp.cos(angle) / scale, -(jnp.sin(angle) / scale)

    bins = after(freq_bins, meta)
    x_at = jnp.arange(parts, dtype=jnp.int32) * 8
    x_in = jnp.arange(8, dtype=jnp.int32)[:, None] + x_at[None, :]
    x_out = (jnp.arange(-4, 12, dtype=jnp.int32)[:, None] + x_at[None, :]).reshape(-1)
    to_data = jnp.concatenate(table(bins[None, :, None] * x_in[:, None, :]), axis=1)
    to_data = to_data.reshape(8 * 32, parts)
    from_data = jnp.concatenate(table(bins[:, None] * x_out[None, :]), axis=0)
    seen = measured.reshape(32, 16)
    meta = after(meta, to_data, from_data)
    nh = halos[0][0].shape[1]

    own, arrived = [], []

    def deep(meta, c):
        terms = deep_call(meta, fwd, adj, absorption, *halos[c], CHUNKS[c])
        if CHUNKS[c][0]:
            arrived.append(lax.ppermute(terms, ALL, pat_pairs))
        else:
            own.append(terms)
        return after(meta, terms)

    meta = deep(meta, 0)
    fsh, surf = vmem_call(
        functools.partial(forward_kernel, ny=ny),
        [(8, 8, ny), (parts, 128)],
        shallow_scratch(ny, nh),
        3,
        2,
    )(meta, t1, t2, src, near, far)
    meta = after(meta, surf)
    got = lax.all_to_all(surf, GX, 0, 0, tiled=True)
    meta = deep(meta, 1)
    model, rows = vmem_call(
        data_kernel, [(32, 128), (parts, 256)], [pltpu.VMEM((32, 128), F32)], 4
    )(
        meta, got, to_data, from_data, seen
    )
    meta = after(meta, rows)
    back = lax.all_to_all(rows, GX, 0, 0, tiled=True)
    send, keep = vmem_call(
        functools.partial(adjoint_kernel, ny=ny),
        [(64, ny // 2), (64, ny // 2)],
        shallow_scratch(ny, nh) + [pltpu.VMEM((64, ny), F32)],
        4,
        2,
    )(meta, t1, t2, back, fsh, near, far)
    meta = after(meta, send)
    recv = lax.ppermute(send, ALL, pat_pairs)
    for c in range(2, len(CHUNKS)):
        meta = deep(meta, c)
    gradient = final_call(own, arrived, keep, recv)
    return (gradient, model[:, :16].reshape(1, 2, 16, 16))


def solution(mesh):
    torus = Mesh(mesh.devices.reshape(mesh.shape["pat"], 4, 2, 4, 2), ALL)
    in_specs = (
        P("pat"),
        P(None, GX, None),
        P(),
        P(GX, None, None),
        P("pat", GX, None, None),
        P("pat", GX, None, None),
        P("pat", None, None, GX),
    )
    out_specs = (P(GX, "pat", None), P("pat", None, None, GX))

    return jax.shard_map(
        shards, mesh=torus, in_specs=in_specs, out_specs=out_specs, check_vma=False
    )
```

```python
import functools
import math

import jax
import jax.numpy as jnp
from jax import lax
from jax.experimental import pallas as pl
from jax.experimental.pallas import tpu as pltpu
from jax.sharding import Mesh
from jax.sharding import PartitionSpec as P

SWEEPS = 4
GX = ("gx_0", "gx_1", "gx_2", "gx_3")
ALL = ("pat",) + GX
CHUNKS = ((True, 0, 256), (True, 256, 256), (False, 0, 512))
HIGH = lax.Precision.HIGHEST
F32 = jnp.float32
BF16 = jnp.bfloat16
MXU_PLANES = (1,)
PLANES = 2


def sweep_weight(sweep):
    return 1.0 / (1.25 + 0.75 * math.cos(math.pi * (2 * sweep + 1) / (2 * SWEEPS)))


def halo_rows(rows, ny):
    return rows + 8 if 2 * rows == ny else rows + 16


def chunk_start(meta_ref, sends, offset, half):
    pat = meta_ref[0]
    which = 1 - pat if sends else pat
    return which * half + offset


def iota(shape, dim):
    return lax.broadcasted_iota(jnp.int32, shape, dim)


def face_copies(meta, bufs, base, near, far, sem, chunk, ny):
    sends, offset, rows = chunk
    nh = halo_rows(rows, ny)
    y0 = chunk_start(meta, sends, offset, ny // 2)
    s = pl.multiple_of(jnp.clip(y0 - 8, 0, ny - nh) - base, 8)
    core = meta[4]
    outs = []
    for k, (arr, at, count) in enumerate(zip(bufs, (0, 4, 8), (4, 4, 3))):
        top = 8 - count
        for i, (dst, x) in enumerate(((far, core * top), (near, (1 - core) * top))):
            cp = pltpu.make_async_copy(
                arr.at[pl.ds(x, count), pl.ds(s, nh), :], dst.at[pl.ds(at, count)], sem.at[i, k]
            )
            cp.start()
            outs.append(cp)
    return outs


SHALLOW_ROWS = 96


def shallow_place(v, row, nh):
    at = SHALLOW_ROWS * v + row
    return at // nh, at % nh


def head_kernel(
    meta, fwd, adj, absn, pats, face0, face1, t1, t2, src, near, far, fs, ad, ab,
    in_sem, src_sem, face_sem, *, chunk, ny
):
    loads = []
    for i, (h, v) in enumerate(((fwd, fs), (adj, ad), (absn, ab))):
        cp = pltpu.make_async_copy(h, v, in_sem.at[i])
        cp.start()
        loads.append(cp)
    src_cp = pltpu.make_async_copy(pats.at[meta[3]], src, src_sem)
    src_cp.start()

    def pack(arr, dst, base):
        def body(x, carry):
            at = pl.multiple_of(base + 8 * x, 8)
            for v in range(ny // 128):
                dst[pl.ds(at, 8), 128 * v : 128 * v + 128] = arr[x, 128 * v : 128 * v + 128, :].T[:8]
            return carry

        lax.fori_loop(0, 8, body, 0)

    loads[0].wait()
    pack(fs, t1, 0)
    loads[1].wait()
    pack(ad, t1, 64)
    loads[2].wait()
    outs = face_copies(meta, (fs, ad, ab), 0, face0, face1, face_sem, chunk, ny)
    pack(ab, t2, 0)
    src_cp.wait()
    nh = near.shape[1]

    def put(dst, value, row):
        for v in range(ny // 128):
            p, r = shallow_place(v, row, nh)
            dst[p, r : r + 8, :] = value[:, 128 * v : 128 * v + 128]

    def high_face(dst):
        for i in range(4):
            put(dst, t1[32 + 8 * i : 40 + 8 * i, :], 8 * i)
            put(dst, t1[96 + 8 * i : 104 + 8 * i, :], 32 + 8 * i)
        for i in range(3):
            put(dst, t2[40 + 8 * i : 48 + 8 * i, :], 64 + 8 * i)
        put(dst, pltpu.roll(src[...], 3, axis=0), 88)

    def low_face(dst):
        for i in range(4):
            put(dst, t1[8 * i : 8 * i + 8, :], 8 * i)
            put(dst, t1[64 + 8 * i : 72 + 8 * i, :], 32 + 8 * i)
        for i in range(3):
            put(dst, t2[8 * i : 8 * i + 8, :], 64 + 8 * i)
        put(dst, src[...], 88)

    @pl.when(meta[4] == 0)
    def _():
        high_face(near)
        low_face(far)

    @pl.when(meta[4] != 0)
    def _():
        low_face(near)
        high_face(far)

    for cp in outs:
        cp.wait()


def head_call(meta, fwd, adj, absn, pats, chunk):
    ny = fwd.shape[1]
    face = (11, halo_rows(chunk[2], ny), 128)
    shallow = (3, SHALLOW_ROWS * ny // 128 // 3, 128)
    shapes = [face, face, (128, ny), (64, ny), (8, ny), shallow, shallow]
    any_spec = pl.BlockSpec(memory_space=pl.ANY)
    vmem = pl.BlockSpec(memory_space=pltpu.VMEM)
    return pl.pallas_call(
        functools.partial(head_kernel, chunk=chunk, ny=ny),
        out_shape=[jax.ShapeDtypeStruct(s, F32) for s in shapes],
        in_specs=[pl.BlockSpec(memory_space=pltpu.SMEM)] + [any_spec] * 4,
        out_specs=[any_spec] * 2 + [vmem] * 5,
        scratch_shapes=[pltpu.VMEM((8, ny, 128), F32)] * 3
        + [
            pltpu.SemaphoreType.DMA((3,)),
            pltpu.SemaphoreType.DMA(()),
            pltpu.SemaphoreType.DMA((2, 3)),
        ],
        name="head",
    )(meta, fwd, adj, absn, pats)


def group_transpose(v):
    row = iota((8, 128), 0)
    group = iota((8, 128), 1) // 16
    for b in (1, 2, 4):
        rb = (row // b) % 2
        gb = (group // b) % 2
        down = pltpu.roll(pltpu.roll(v, b, axis=0), 128 - 16 * b, axis=1)
        upw = pltpu.roll(pltpu.roll(v, 8 - b, axis=0), 16 * b, axis=1)
        v = jnp.where(rb == gb, v, jnp.where(rb == 1, down, upw))
    return v


def shallow_side(near, far, core0, row, ny):
    a, b = [], []
    for v in range(ny // 128):
        p, r = shallow_place(v, row, near.shape[1])
        a.append(near[p, r : r + 8, :])
        b.append(far[p, r : r + 8, :])
    a = jnp.concatenate(a, axis=1)
    b = jnp.concatenate(b, axis=1)
    return jnp.where(core0, b, a), jnp.where(core0, a, b)


def shallow_solve(meta, start, at, near, far, near_at, t2, f0, f1, r, s, ny, midway=None):
    lo_ok = jnp.where(meta[1] > 0, 1.0, 0.0).astype(F32)
    hi_ok = jnp.where(meta[2] > 0, 1.0, 0.0).astype(F32)
    core0 = meta[4] == 0

    def side(row):
        return shallow_side(near, far, core0, row, ny)

    for i in range(4):
        f0[i], f0[12 + i] = side(near_at + 8 * i)
    for i in range(8):
        f0[4 + i] = start[at + 8 * i : at + 8 * i + 8, :]
        r[4 + i] = 1.0 / (6.0 + t2[8 * i : 8 * i + 8, :])
    for i in range(3):
        lo, hi = side(64 + 8 * i)
        r[1 + i] = lo_ok / (6.0 + lo)
        r[12 + i] = hi_ok / (6.0 + hi)
    zi = iota((8, ny), 0)
    yi = iota((8, ny), 1)
    bufs = (f0, f1)
    for k in range(SWEEPS):
        w = sweep_weight(k)
        old, new = bufs[k % 2], bufs[1 - k % 2]
        if k == 2 and midway is not None:
            midway()

        def pair(q, carry, old=old, new=new, w=w, k=k):
            p = k + 1 + 2 * q
            v = [old[p - 1 + i] for i in range(4)]
            for i in range(2):
                c = v[i + 1]
                nb = v[i] + v[i + 2]
                nb = nb + jnp.where(yi == 0, 0.0, pltpu.roll(c, 1, axis=1))
                nb = nb + jnp.where(yi == ny - 1, 0.0, pltpu.roll(c, ny - 1, axis=1))
                nb = nb + jnp.where(zi == 0, 0.0, pltpu.roll(c, 1, axis=0))
                nb = nb + jnp.where(zi == 7, 0.0, pltpu.roll(c, 7, axis=0))
                new[p + i] = (1.0 - w) * c + (w * r[p + i]) * (nb + s[p + i])
            return carry

        lax.fori_loop(0, 7 - k, pair, 0)


def forward_kernel(meta, t1, t2, src, near, far, fwd, adj, absn, fsh, surf, *rest, chunks, ny):
    n = 2 * len(chunks)
    faces = rest[:n]
    f0, f1, r, s, fs, ad, ab, in_sem, face_sem = rest[n:]
    loads = []
    for i, (h, v) in enumerate(((fwd, fs), (adj, ad), (absn, ab))):
        cp = pltpu.make_async_copy(h, v, in_sem.at[i])
        cp.start()
        loads.append(cp)
    outs = []

    def midway():
        for cp in loads:
            cp.wait()
        for c, chunk in enumerate(chunks):
            outs.extend(
                face_copies(
                    meta, (fs, ad, ab), 0, faces[2 * c], faces[2 * c + 1], face_sem.at[c], chunk, ny
                )
            )

    z0 = iota((8, ny), 0) == 0
    lo, hi = shallow_side(near, far, meta[4] == 0, 88, ny)
    for i in range(3):
        s[1 + i] = jnp.where(z0, lo[i : i + 1, :], 0.0)
        s[12 + i] = jnp.where(z0, hi[i : i + 1, :], 0.0)
    for i in range(8):
        s[4 + i] = jnp.where(z0, src[i : i + 1, :], 0.0)
    shallow_solve(meta, t1, 0, near, far, 0, t2, f0, f1, r, s, ny, midway)
    for i in range(8):
        fsh[i] = f0[4 + i]
    top = jnp.concatenate([f0[4 + i, 0:1, :] for i in range(8)], axis=0)
    for v in range(ny // 128):
        surf[8 * v : 8 * v + 8, :] = group_transpose(top[:, 128 * v : 128 * v + 128])
    for cp in outs:
        cp.wait()


def forward_call(meta, t1, t2, src, near, far, fwd, adj, absn, chunks):
    ny = fwd.shape[1]
    any_spec = pl.BlockSpec(memory_space=pl.ANY)
    vmem = pl.BlockSpec(memory_space=pltpu.VMEM)
    shapes = [(8, 8, ny), (ny // 16, 128)]
    for _, _, rows in chunks:
        shapes += [(11, halo_rows(rows, ny), 128)] * 2
    return pl.pallas_call(
        functools.partial(forward_kernel, chunks=chunks, ny=ny),
        out_shape=[jax.ShapeDtypeStruct(s, F32) for s in shapes],
        in_specs=[pl.BlockSpec(memory_space=pltpu.SMEM)] + [vmem] * 5 + [any_spec] * 3,
        out_specs=[vmem] * 2 + [any_spec] * (2 * len(chunks)),
        scratch_shapes=shallow_scratch(ny)
        + [pltpu.VMEM((8, ny, 128), F32)] * 3
        + [pltpu.SemaphoreType.DMA((3,)), pltpu.SemaphoreType.DMA((len(chunks), 2, 3))],
        name="shallow_forward",
    )(meta, t1, t2, src, near, far, fwd, adj, absn)


def shallow_scratch(ny):
    return [pltpu.VMEM((16, 8, ny), F32)] * 4


def vmem_call(kernel, out_shapes, scratch, n_in, n_any=0):
    vmem = pl.BlockSpec(memory_space=pltpu.VMEM)
    any_spec = pl.BlockSpec(memory_space=pl.ANY)
    return pl.pallas_call(
        kernel,
        out_shape=[jax.ShapeDtypeStruct(s, F32) for s in out_shapes],
        in_specs=[pl.BlockSpec(memory_space=pltpu.SMEM)] + [vmem] * n_in + [any_spec] * n_any,
        out_specs=[vmem] * len(out_shapes),
        scratch_shapes=scratch,
    )


def adjoint_kernel(
    meta, t1, t2, got, near, far, fsh, send, keep, f0, f1, r, s, prod, *, ny
):
    z0 = iota((8, ny), 0) == 0
    for h in range(2):
        parts = []
        for v in range(ny // 128):
            parts.append(group_transpose(got[8 * v : 8 * v + 8, 128 * h : 128 * h + 128]))
        rows = jnp.concatenate(parts, axis=1)
        for j in range(8):
            s[8 * h + j] = jnp.where(z0, rows[j : j + 1, :], 0.0)
    shallow_solve(meta, t1, 64, near, far, 32, t2, f0, f1, r, s, ny)
    for i in range(8):
        prod[8 * i : 8 * i + 8, :] = -(fsh[i] * f0[4 + i])
    half = ny // 2

    @pl.when(meta[0] == 0)
    def _():
        keep[...] = prod[:, :half]
        send[...] = prod[:, half:]

    @pl.when(meta[0] != 0)
    def _():
        keep[...] = prod[:, half:]
        send[...] = prod[:, :half]


def data_kernel(meta, got, table, back, measured, model, send, seen):
    lane_group = iota((32, 128), 1) // 16
    full = jnp.dot(table[...], got[...], precision=HIGH, preferred_element_type=F32)
    acc = jnp.zeros((32, 128), F32)
    for x in range(8):
        acc = acc + jnp.where(lane_group == x, full[32 * x : 32 * x + 32, :], 0.0)
    for shift in (64, 32, 16):
        acc = acc + pltpu.roll(acc, shift, axis=1)
    model[...] = acc
    seen[...] = jnp.zeros((32, 128), F32)
    seen[:, :16] = measured[...]
    data = seen[...]
    for shift in (16, 32, 64):
        data = data + pltpu.roll(data, shift, axis=1)
    misfit = acc - data
    rows = lax.dot_general(
        back[...], misfit, (((0,), (0,)), ((), ())), precision=HIGH, preferred_element_type=F32
    )
    count = rows.shape[0] // 16
    group = iota((count, 128), 1) // 16
    for h in range(2):
        out = jnp.zeros((count, 128), F32)
        for j in range(8):
            at = (8 * h + j) * count
            out = jnp.where(group == j, rows[at : at + count, :], out)
        send[:, 128 * h : 128 * h + 128] = out


def tile_count(tiles, most=66):
    return max(u for u in range(1, most + 1) if tiles % u == 0)


def deep_kernel(
    meta, fwd, adj, absn, near, far, out, f0, f1, a0, a1, rb, zb, sem, *, sends, offset, rows, ny
):
    nh = halo_rows(rows, ny)
    y0 = chunk_start(meta, sends, offset, ny // 2)
    s = pl.multiple_of(jnp.clip(y0 - 8, 0, ny - nh), 8)
    off = pl.multiple_of(s - y0 + 16, 8)
    core = meta[4]

    def group(arr, at, count, buf, k):
        below = 4 - count
        cps = [
            pltpu.make_async_copy(
                arr.at[:, pl.ds(s, nh), :], buf.at[pl.ds(4, 8), pl.ds(off, nh), :], sem.at[k, 0]
            ),
            pltpu.make_async_copy(
                near.at[pl.ds(at, count)],
                buf.at[pl.ds(jnp.where(core == 0, 12, below), count), pl.ds(off, nh), :],
                sem.at[k, 1],
            ),
            pltpu.make_async_copy(
                far.at[pl.ds(at, count)],
                buf.at[pl.ds(jnp.where(core == 0, below, 12), count), pl.ds(off, nh), :],
                sem.at[k, 2],
            ),
        ]
        for cp in cps:
            cp.start()
        return cps

    r_cps = group(absn, 8, 3, rb, 0)
    f_cps = group(fwd, 0, 4, f0, 1)
    a_cps = group(adj, 4, 4, a0, 2)
    zero = jnp.zeros((16, 8, 128), F32)

    def edges(buf):
        @pl.when(y0 == 0)
        def _():
            buf[:, 8:16, :] = zero

        @pl.when(y0 + rows == ny)
        def _():
            buf[:, rows + 16 : rows + 24, :] = zero

    edges(f0)
    edges(a0)
    tiles = (rows + 16) // 8
    for cp in r_cps:
        cp.wait()

    def invert(p, carry):
        ok = jnp.where(p < 4, meta[1], jnp.where(p >= 12, meta[2], 1))
        ok = jnp.where(ok > 0, 1.0, 0.0).astype(F32)
        un = tile_count(tiles)

        def block(t, c):
            ys = [pl.multiple_of(8 + (t * un + u) * 8, 8) for u in range(un)]
            new = [ok / (6.0 + rb[p, pl.ds(y, 8), :]) for y in ys]
            for y, v in zip(ys, new):
                rb[p, pl.ds(y, 8), :] = v
            return c

        return lax.fori_loop(0, tiles // un, block, carry)

    lax.fori_loop(1, 15, invert, 0)
    edges(rb)
    last = iota((8, 128), 1) == 127
    apart = jnp.abs(iota((128, 128), 0) - iota((128, 128), 1))
    shifts = jnp.where(apart == 1, 1.0, 0.0).astype(BF16)
    shifts = jnp.concatenate([shifts, shifts], axis=0)

    def sweep(buf, k, begin, count, store):
        w = sweep_weight(k)

        def pair(q, carry):
            p = k + 1 + 2 * q
            for i in MXU_PLANES:
                c = buf[p + i, begin : begin + 8 * count, :]
                head = c.astype(BF16)
                tail = (c - head.astype(F32)).astype(BF16)
                both = jnp.concatenate([head, tail], axis=1)
                zb[i, : 8 * count, :] = jnp.dot(both, shifts, preferred_element_type=F32)
            for t in range(count):
                y = begin + 8 * t
                v = [buf[p - 1 + i, y : y + 8, :] for i in range(4)]
                for i in range(2):
                    ym = buf[p + i, y - 1 : y + 7, :]
                    yp = buf[p + i, y + 1 : y + 9, :]
                    if i in MXU_PLANES:
                        zs = zb[i, 8 * t : 8 * t + 8, :]
                    else:
                        zr = jnp.where(last, 0.0, pltpu.roll(v[i + 1], 127, axis=1))
                        zs = pltpu.roll(v[i + 1], 1, axis=1) + zr
                    nb = ((v[i] + v[i + 2]) + (ym + yp)) + zs
                    store(p + i, y, ((1.0 - w) / w) * v[i + 1] + rb[p + i, y : y + 8, :] * nb)
            return carry

        lax.fori_loop(0, 7 - k, pair, 0)

    def into(buf):
        def store(p, y, new):
            buf[p, y : y + 8, :] = new

        return store

    scale = -math.prod(sweep_weight(k) for k in range(SWEEPS)) ** 2

    def product(p, y, new):
        out[p - 4, y - 16 : y - 8, :] = (scale * f0[p, y : y + 8, :]) * new

    for bufs, cps in (((f0, f1), f_cps), ((a0, a1), a_cps)):
        for cp in cps:
            cp.wait()
        for k in range(SWEEPS):
            src, dst = bufs[k % 2], bufs[1 - k % 2]
            if k < SWEEPS - 1:
                sweep(src, k, 8, tiles, into(dst))
            elif src is f1:
                sweep(src, k, 16, rows // 8, into(dst))
            else:
                sweep(src, k, 16, rows // 8, product)


def deep_call(meta, fwd, adj, absn, near, far, chunk):
    sends, offset, rows = chunk
    ny = fwd.shape[1]
    any_spec = pl.BlockSpec(memory_space=pl.ANY)
    return pl.pallas_call(
        functools.partial(deep_kernel, sends=sends, offset=offset, rows=rows, ny=ny),
        out_shape=jax.ShapeDtypeStruct((8, rows, 128), F32),
        in_specs=[pl.BlockSpec(memory_space=pltpu.SMEM)] + [any_spec] * 5,
        out_specs=pl.BlockSpec(memory_space=pltpu.VMEM),
        scratch_shapes=[
            pltpu.VMEM((16, rows + 32, 128), F32),
            pltpu.VMEM((16, rows + 32, 128), F32),
            pltpu.VMEM((16, rows + 32, 128), F32),
            pltpu.VMEM((16, rows + 32, 128), F32),
            pltpu.VMEM((16, rows + 32, 128), F32),
            pltpu.VMEM((2, rows + 16, 128), F32),
            pltpu.SemaphoreType.DMA((3, 3)),
        ],
    )(meta, fwd, adj, absn, near, far)


def final_kernel(*refs, n_own, n_got):
    own = refs[:n_own]
    got = refs[n_own : n_own + n_got]
    keep, recv, out, packed = refs[n_own + n_got :]
    x = pl.program_id(0)

    @pl.when(x == 0)
    def _():
        both = keep[...] + recv[...]
        for v in range(both.shape[1] // 128):
            cols = both[:, 128 * v : 128 * v + 128]
            cols = jnp.concatenate([cols, cols], axis=0)
            packed[128 * v : 128 * v + 128, :] = cols.T

    def cover(parts):
        at = 0
        found = []
        for ref in parts:
            found.append((at, ref.shape[1], ref))
            at += ref.shape[1]
        return found

    cuts = sorted({a for a, _, _ in cover(own)} | {a for a, _, _ in cover(got)} | {out.shape[1]})

    def piece(parts, a, b, i):
        for at, size, ref in cover(parts):
            if at <= a and b <= at + size:
                return ref[i, a - at : b - at, :]

    for a, b in zip(cuts[:-1], cuts[1:]):
        for i in range(PLANES):
            shift = (128 - 8 * (PLANES * x + i)) % 128
            shallow = pltpu.roll(packed[a:b, :], shift, axis=1)
            deep = piece(own, a, b, i) + piece(got, a, b, i)
            out[i, a:b, :] = jnp.where(iota((b - a, 128), 1) < 4, shallow, deep)


def final_call(own, got, keep, recv):
    half = keep.shape[1]

    def spec(a):
        return pl.BlockSpec((PLANES, a.shape[1], 128), lambda x: (x, 0, 0))

    whole = pl.BlockSpec((64, half), lambda x: (0, 0))
    return pl.pallas_call(
        functools.partial(final_kernel, n_own=len(own), n_got=len(got)),
        out_shape=jax.ShapeDtypeStruct((8, half, 128), F32),
        grid=(8 // PLANES,),
        in_specs=[spec(a) for a in own + got] + [whole, whole],
        out_specs=pl.BlockSpec((PLANES, half, 128), lambda x: (x, 0, 0)),
        scratch_shapes=[pltpu.VMEM((half, 128), F32)],
        name="final",
    )(*own, *got, keep, recv)


def after(value, *others):
    return lax.optimization_barrier((value, others))[0]


def shards(pattern_index, patterns, freq_bins, absorption, forward_start, adjoint_start, measured):
    ny = forward_start.shape[2]
    parts = lax.axis_size(GX)
    total_x = parts * 8
    fwd = forward_start[0]
    adj = adjoint_start[0]
    gx = lax.axis_index(GX)
    meta = jnp.stack(
        [
            lax.axis_index("pat"),
            (gx > 0).astype(jnp.int32),
            (gx < parts - 1).astype(jnp.int32),
            pattern_index[0],
            gx % 2,
        ]
    ).astype(jnp.int32)

    lid = [[p * parts + g for g in range(parts)] for p in range(2)]
    near_pairs = [(r[g], r[g ^ 1]) for r in lid for g in range(parts)]
    far_pairs = []
    for r in lid:
        for g in range(1, parts - 1, 2):
            far_pairs += [(r[g], r[g + 1]), (r[g + 1], r[g])]
    pat_pairs = [(lid[p][g], lid[1 - p][g]) for p in range(2) for g in range(parts)]

    def exchange(near, far):
        near = lax.ppermute(near, ALL, near_pairs)
        far = lax.ppermute(far, ALL, far_pairs)
        return near, far

    out = head_call(meta, fwd, adj, absorption, patterns, CHUNKS[0])
    t1, t2, src = out[2:5]
    near, far = exchange(out[5], out[6])
    halos = [exchange(out[0], out[1])]
    meta = after(meta, t1)

    def table(phase):
        angle = 2.0 * math.pi / total_x * (phase % total_x).astype(F32)
        scale = math.sqrt(total_x)
        return jnp.cos(angle) / scale, -(jnp.sin(angle) / scale)

    bins = after(freq_bins, meta)
    x_at = jnp.arange(parts, dtype=jnp.int32) * 8
    x_in = jnp.arange(8, dtype=jnp.int32)[:, None] + x_at[None, :]
    x_out = (jnp.arange(-4, 12, dtype=jnp.int32)[:, None] + x_at[None, :]).reshape(-1)
    to_data = jnp.concatenate(table(bins[None, :, None] * x_in[:, None, :]), axis=1)
    to_data = to_data.reshape(8 * 32, parts)
    from_data = jnp.concatenate(table(bins[:, None] * x_out[None, :]), axis=0)
    seen = measured.reshape(32, 16)
    meta = after(meta, to_data, from_data)

    own, arrived = [], []

    def deep(meta, c):
        terms = deep_call(meta, fwd, adj, absorption, *halos[c], CHUNKS[c])
        if CHUNKS[c][0]:
            arrived.append(lax.ppermute(terms, ALL, pat_pairs))
        else:
            own.append(terms)
        return after(meta, terms)

    fsh, surf, *faces = forward_call(meta, t1, t2, src, near, far, fwd, adj, absorption, CHUNKS[1:])
    meta = after(meta, surf)
    got = lax.all_to_all(surf, GX, 0, 0, tiled=True)
    for c in range(1, len(CHUNKS)):
        halos.append(exchange(faces[2 * c - 2], faces[2 * c - 1]))
    model, rows = vmem_call(
        data_kernel, [(32, 128), (parts, 256)], [pltpu.VMEM((32, 128), F32)], 4
    )(meta, got, to_data, from_data, seen)
    meta = after(meta, rows)
    back = lax.all_to_all(rows, GX, 0, 0, tiled=True)
    meta = deep(meta, 0)
    meta = deep(meta, 1)
    send, keep = vmem_call(
        functools.partial(adjoint_kernel, ny=ny),
        [(64, ny // 2), (64, ny // 2)],
        shallow_scratch(ny) + [pltpu.VMEM((64, ny), F32)],
        6,
    )(meta, t1, t2, back, near, far, fsh)
    meta = after(meta, send)
    recv = lax.ppermute(send, ALL, pat_pairs)
    for c in range(2, len(CHUNKS)):
        meta = deep(meta, c)
    gradient = final_call(own, arrived, keep, recv)
    return (gradient, model[:, :16].reshape(1, 2, 16, 16))


def solution(mesh):
    torus = Mesh(mesh.devices.reshape(mesh.shape["pat"], 4, 2, 4, 2), ALL)
    in_specs = (
        P("pat"),
        P(None, GX, None),
        P(),
        P(GX, None, None),
        P("pat", GX, None, None),
        P("pat", GX, None, None),
        P("pat", None, None, GX),
    )
    out_specs = (P(GX, "pat", None), P("pat", None, None, GX))

    return jax.shard_map(
        shards, mesh=torus, in_specs=in_specs, out_specs=out_specs, check_vma=False
    )
```

```python
import functools
import math

import jax
import jax.numpy as jnp
from jax import lax
from jax.experimental import pallas as pl
from jax.experimental.pallas import tpu as pltpu
from jax.sharding import Mesh
from jax.sharding import PartitionSpec as P

SWEEPS = 4
GX = ("gx_0", "gx_1", "gx_2", "gx_3")
ALL = ("pat",) + GX
CHUNKS = ((True, 0, 256), (True, 256, 256), (False, 0, 512))
HIGH = lax.Precision.HIGHEST
F32 = jnp.float32
BF16 = jnp.bfloat16
MXU_PLANES = (1,)
PLANES = 2
EARLY = 2


def sweep_weight(sweep):
    return 1.0 / (1.25 + 0.75 * math.cos(math.pi * (2 * sweep + 1) / (2 * SWEEPS)))


def halo_rows(rows, ny):
    return rows + 8 if 2 * rows == ny else rows + 16


def chunk_start(meta_ref, sends, offset, half):
    pat = meta_ref[0]
    which = 1 - pat if sends else pat
    return which * half + offset


def iota(shape, dim):
    return lax.broadcasted_iota(jnp.int32, shape, dim)


def face_copies(meta, bufs, base, near, far, sem, chunk, ny):
    sends, offset, rows = chunk
    nh = halo_rows(rows, ny)
    y0 = chunk_start(meta, sends, offset, ny // 2)
    s = pl.multiple_of(jnp.clip(y0 - 8, 0, ny - nh) - base, 8)
    core = meta[4]
    outs = []
    for k, (arr, at, count) in enumerate(zip(bufs, (0, 4, 8), (4, 4, 3))):
        top = 8 - count
        for i, (dst, x) in enumerate(((far, core * top), (near, (1 - core) * top))):
            cp = pltpu.make_async_copy(
                arr.at[pl.ds(x, count), pl.ds(s, nh), :], dst.at[pl.ds(at, count)], sem.at[i, k]
            )
            cp.start()
            outs.append(cp)
    return outs


SHALLOW_ROWS = 96


def shallow_place(v, row, nh):
    at = SHALLOW_ROWS * v + row
    return at // nh, at % nh


def head_kernel(
    meta, fwd, adj, absn, pats, *rest, chunks, ny
):
    n = 2 * len(chunks)
    faces = rest[:n]
    t1, t2, src, near, far, fs, ad, ab, in_sem, src_sem, face_sem = rest[n:]
    loads = []
    for i, (h, v) in enumerate(((fwd, fs), (adj, ad), (absn, ab))):
        cp = pltpu.make_async_copy(h, v, in_sem.at[i])
        cp.start()
        loads.append(cp)
    src_cp = pltpu.make_async_copy(pats.at[meta[3]], src, src_sem)
    src_cp.start()

    def pack(arr, dst, base):
        def body(x, carry):
            at = pl.multiple_of(base + 8 * x, 8)
            for v in range(ny // 128):
                dst[pl.ds(at, 8), 128 * v : 128 * v + 128] = arr[x, 128 * v : 128 * v + 128, :].T[:8]
            return carry

        lax.fori_loop(0, 8, body, 0)

    loads[0].wait()
    pack(fs, t1, 0)
    loads[1].wait()
    pack(ad, t1, 64)
    loads[2].wait()
    outs = []
    for c, chunk in enumerate(chunks):
        outs += face_copies(
            meta, (fs, ad, ab), 0, faces[2 * c], faces[2 * c + 1], face_sem.at[c], chunk, ny
        )
    pack(ab, t2, 0)
    src_cp.wait()
    nh = near.shape[1]

    def put(dst, value, row):
        for v in range(ny // 128):
            p, r = shallow_place(v, row, nh)
            dst[p, r : r + 8, :] = value[:, 128 * v : 128 * v + 128]

    def high_face(dst):
        for i in range(4):
            put(dst, t1[32 + 8 * i : 40 + 8 * i, :], 8 * i)
            put(dst, t1[96 + 8 * i : 104 + 8 * i, :], 32 + 8 * i)
        for i in range(3):
            put(dst, t2[40 + 8 * i : 48 + 8 * i, :], 64 + 8 * i)
        put(dst, pltpu.roll(src[...], 3, axis=0), 88)

    def low_face(dst):
        for i in range(4):
            put(dst, t1[8 * i : 8 * i + 8, :], 8 * i)
            put(dst, t1[64 + 8 * i : 72 + 8 * i, :], 32 + 8 * i)
        for i in range(3):
            put(dst, t2[8 * i : 8 * i + 8, :], 64 + 8 * i)
        put(dst, src[...], 88)

    @pl.when(meta[4] == 0)
    def _():
        high_face(near)
        low_face(far)

    @pl.when(meta[4] != 0)
    def _():
        low_face(near)
        high_face(far)

    for cp in outs:
        cp.wait()


def head_call(meta, fwd, adj, absn, pats, chunks):
    ny = fwd.shape[1]
    shallow = (3, SHALLOW_ROWS * ny // 128 // 3, 128)
    shapes = []
    for _, _, rows in chunks:
        shapes += [(11, halo_rows(rows, ny), 128)] * 2
    shapes += [(128, ny), (64, ny), (8, ny), shallow, shallow]
    any_spec = pl.BlockSpec(memory_space=pl.ANY)
    vmem = pl.BlockSpec(memory_space=pltpu.VMEM)
    return pl.pallas_call(
        functools.partial(head_kernel, chunks=chunks, ny=ny),
        out_shape=[jax.ShapeDtypeStruct(s, F32) for s in shapes],
        in_specs=[pl.BlockSpec(memory_space=pltpu.SMEM)] + [any_spec] * 4,
        out_specs=[any_spec] * (2 * len(chunks)) + [vmem] * 5,
        scratch_shapes=[pltpu.VMEM((8, ny, 128), F32)] * 3
        + [
            pltpu.SemaphoreType.DMA((3,)),
            pltpu.SemaphoreType.DMA(()),
            pltpu.SemaphoreType.DMA((len(chunks), 2, 3)),
        ],
        name="head",
    )(meta, fwd, adj, absn, pats)


def group_transpose(v):
    row = iota((8, 128), 0)
    group = iota((8, 128), 1) // 16
    for b in (1, 2, 4):
        rb = (row // b) % 2
        gb = (group // b) % 2
        down = pltpu.roll(pltpu.roll(v, b, axis=0), 128 - 16 * b, axis=1)
        upw = pltpu.roll(pltpu.roll(v, 8 - b, axis=0), 16 * b, axis=1)
        v = jnp.where(rb == gb, v, jnp.where(rb == 1, down, upw))
    return v


def shallow_side(near, far, core0, row, ny):
    a, b = [], []
    for v in range(ny // 128):
        p, r = shallow_place(v, row, near.shape[1])
        a.append(near[p, r : r + 8, :])
        b.append(far[p, r : r + 8, :])
    a = jnp.concatenate(a, axis=1)
    b = jnp.concatenate(b, axis=1)
    return jnp.where(core0, b, a), jnp.where(core0, a, b)


def shallow_solve(meta, start, at, near, far, near_at, t2, f0, f1, r, s, ny, midway=None):
    lo_ok = jnp.where(meta[1] > 0, 1.0, 0.0).astype(F32)
    hi_ok = jnp.where(meta[2] > 0, 1.0, 0.0).astype(F32)
    core0 = meta[4] == 0

    def side(row):
        return shallow_side(near, far, core0, row, ny)

    for i in range(4):
        f0[i], f0[12 + i] = side(near_at + 8 * i)
    for i in range(8):
        f0[4 + i] = start[at + 8 * i : at + 8 * i + 8, :]
        r[4 + i] = 1.0 / (6.0 + t2[8 * i : 8 * i + 8, :])
    for i in range(3):
        lo, hi = side(64 + 8 * i)
        r[1 + i] = lo_ok / (6.0 + lo)
        r[12 + i] = hi_ok / (6.0 + hi)
    zi = iota((8, ny), 0)
    yi = iota((8, ny), 1)
    bufs = (f0, f1)
    for k in range(SWEEPS):
        w = sweep_weight(k)
        old, new = bufs[k % 2], bufs[1 - k % 2]
        if k == 2 and midway is not None:
            midway()

        def pair(q, carry, old=old, new=new, w=w, k=k):
            p = k + 1 + 2 * q
            v = [old[p - 1 + i] for i in range(4)]
            for i in range(2):
                c = v[i + 1]
                nb = v[i] + v[i + 2]
                nb = nb + jnp.where(yi == 0, 0.0, pltpu.roll(c, 1, axis=1))
                nb = nb + jnp.where(yi == ny - 1, 0.0, pltpu.roll(c, ny - 1, axis=1))
                nb = nb + jnp.where(zi == 0, 0.0, pltpu.roll(c, 1, axis=0))
                nb = nb + jnp.where(zi == 7, 0.0, pltpu.roll(c, 7, axis=0))
                new[p + i] = (1.0 - w) * c + (w * r[p + i]) * (nb + s[p + i])
            return carry

        lax.fori_loop(0, 7 - k, pair, 0)


def forward_kernel(meta, t1, t2, src, near, far, fwd, adj, absn, fsh, surf, *rest, chunks, ny):
    n = 2 * len(chunks)
    faces = rest[:n]
    f0, f1, r, s, fs, ad, ab, in_sem, face_sem = rest[n:]
    loads = []
    for i, (h, v) in enumerate(((fwd, fs), (adj, ad), (absn, ab))):
        cp = pltpu.make_async_copy(h, v, in_sem.at[i])
        cp.start()
        loads.append(cp)
    outs = []

    def midway():
        for cp in loads:
            cp.wait()
        for c, chunk in enumerate(chunks):
            outs.extend(
                face_copies(
                    meta, (fs, ad, ab), 0, faces[2 * c], faces[2 * c + 1], face_sem.at[c], chunk, ny
                )
            )

    z0 = iota((8, ny), 0) == 0
    lo, hi = shallow_side(near, far, meta[4] == 0, 88, ny)
    for i in range(3):
        s[1 + i] = jnp.where(z0, lo[i : i + 1, :], 0.0)
        s[12 + i] = jnp.where(z0, hi[i : i + 1, :], 0.0)
    for i in range(8):
        s[4 + i] = jnp.where(z0, src[i : i + 1, :], 0.0)
    shallow_solve(meta, t1, 0, near, far, 0, t2, f0, f1, r, s, ny, midway)
    for i in range(8):
        fsh[i] = f0[4 + i]
    top = jnp.concatenate([f0[4 + i, 0:1, :] for i in range(8)], axis=0)
    for v in range(ny // 128):
        surf[8 * v : 8 * v + 8, :] = group_transpose(top[:, 128 * v : 128 * v + 128])
    for cp in outs:
        cp.wait()


def forward_call(meta, t1, t2, src, near, far, fwd, adj, absn, chunks):
    ny = fwd.shape[1]
    any_spec = pl.BlockSpec(memory_space=pl.ANY)
    vmem = pl.BlockSpec(memory_space=pltpu.VMEM)
    shapes = [(8, 8, ny), (ny // 16, 128)]
    for _, _, rows in chunks:
        shapes += [(11, halo_rows(rows, ny), 128)] * 2
    return pl.pallas_call(
        functools.partial(forward_kernel, chunks=chunks, ny=ny),
        out_shape=[jax.ShapeDtypeStruct(s, F32) for s in shapes],
        in_specs=[pl.BlockSpec(memory_space=pltpu.SMEM)] + [vmem] * 5 + [any_spec] * 3,
        out_specs=[vmem] * 2 + [any_spec] * (2 * len(chunks)),
        scratch_shapes=shallow_scratch(ny)
        + [pltpu.VMEM((8, ny, 128), F32)] * 3
        + [pltpu.SemaphoreType.DMA((3,)), pltpu.SemaphoreType.DMA((len(chunks), 2, 3))],
        name="shallow_forward",
    )(meta, t1, t2, src, near, far, fwd, adj, absn)


def shallow_scratch(ny):
    return [pltpu.VMEM((16, 8, ny), F32)] * 4


def vmem_call(kernel, out_shapes, scratch, n_in, n_any=0):
    vmem = pl.BlockSpec(memory_space=pltpu.VMEM)
    any_spec = pl.BlockSpec(memory_space=pl.ANY)
    return pl.pallas_call(
        kernel,
        out_shape=[jax.ShapeDtypeStruct(s, F32) for s in out_shapes],
        in_specs=[pl.BlockSpec(memory_space=pltpu.SMEM)] + [vmem] * n_in + [any_spec] * n_any,
        out_specs=[vmem] * len(out_shapes),
        scratch_shapes=scratch,
    )


def adjoint_kernel(
    meta, t1, t2, got, near, far, fsh, send, keep, f0, f1, r, s, prod, *, ny
):
    z0 = iota((8, ny), 0) == 0
    for h in range(2):
        parts = []
        for v in range(ny // 128):
            parts.append(group_transpose(got[8 * v : 8 * v + 8, 128 * h : 128 * h + 128]))
        rows = jnp.concatenate(parts, axis=1)
        for j in range(8):
            s[8 * h + j] = jnp.where(z0, rows[j : j + 1, :], 0.0)
    shallow_solve(meta, t1, 64, near, far, 32, t2, f0, f1, r, s, ny)
    for i in range(8):
        prod[8 * i : 8 * i + 8, :] = -(fsh[i] * f0[4 + i])
    half = ny // 2

    @pl.when(meta[0] == 0)
    def _():
        keep[...] = prod[:, :half]
        send[...] = prod[:, half:]

    @pl.when(meta[0] != 0)
    def _():
        keep[...] = prod[:, half:]
        send[...] = prod[:, :half]


def data_kernel(meta, got, table, back, measured, model, send, seen):
    lane_group = iota((32, 128), 1) // 16
    full = jnp.dot(table[...], got[...], precision=HIGH, preferred_element_type=F32)
    acc = jnp.zeros((32, 128), F32)
    for x in range(8):
        acc = acc + jnp.where(lane_group == x, full[32 * x : 32 * x + 32, :], 0.0)
    for shift in (64, 32, 16):
        acc = acc + pltpu.roll(acc, shift, axis=1)
    model[...] = acc
    seen[...] = jnp.zeros((32, 128), F32)
    seen[:, :16] = measured[...]
    data = seen[...]
    for shift in (16, 32, 64):
        data = data + pltpu.roll(data, shift, axis=1)
    misfit = acc - data
    rows = lax.dot_general(
        back[...], misfit, (((0,), (0,)), ((), ())), precision=HIGH, preferred_element_type=F32
    )
    count = rows.shape[0] // 16
    group = iota((count, 128), 1) // 16
    for h in range(2):
        out = jnp.zeros((count, 128), F32)
        for j in range(8):
            at = (8 * h + j) * count
            out = jnp.where(group == j, rows[at : at + count, :], out)
        send[:, 128 * h : 128 * h + 128] = out


def tile_count(tiles, most=66):
    return max(u for u in range(1, most + 1) if tiles % u == 0)


def deep_kernel(
    meta, fwd, adj, absn, near, far, out, f0, f1, a0, a1, rb, zb, sem, *, sends, offset, rows, ny
):
    nh = halo_rows(rows, ny)
    y0 = chunk_start(meta, sends, offset, ny // 2)
    s = pl.multiple_of(jnp.clip(y0 - 8, 0, ny - nh), 8)
    off = pl.multiple_of(s - y0 + 16, 8)
    core = meta[4]

    def group(arr, at, count, buf, k):
        below = 4 - count
        cps = [
            pltpu.make_async_copy(
                arr.at[:, pl.ds(s, nh), :], buf.at[pl.ds(4, 8), pl.ds(off, nh), :], sem.at[k, 0]
            ),
            pltpu.make_async_copy(
                near.at[pl.ds(at, count)],
                buf.at[pl.ds(jnp.where(core == 0, 12, below), count), pl.ds(off, nh), :],
                sem.at[k, 1],
            ),
            pltpu.make_async_copy(
                far.at[pl.ds(at, count)],
                buf.at[pl.ds(jnp.where(core == 0, below, 12), count), pl.ds(off, nh), :],
                sem.at[k, 2],
            ),
        ]
        for cp in cps:
            cp.start()
        return cps

    r_cps = group(absn, 8, 3, rb, 0)
    f_cps = group(fwd, 0, 4, f0, 1)
    a_cps = group(adj, 4, 4, a0, 2)
    zero = jnp.zeros((16, 8, 128), F32)

    def edges(buf):
        @pl.when(y0 == 0)
        def _():
            buf[:, 8:16, :] = zero

        @pl.when(y0 + rows == ny)
        def _():
            buf[:, rows + 16 : rows + 24, :] = zero

    edges(f0)
    edges(a0)
    tiles = (rows + 16) // 8
    for cp in r_cps:
        cp.wait()

    def invert(p, carry):
        ok = jnp.where(p < 4, meta[1], jnp.where(p >= 12, meta[2], 1))
        ok = jnp.where(ok > 0, 1.0, 0.0).astype(F32)
        un = tile_count(tiles)

        def block(t, c):
            ys = [pl.multiple_of(8 + (t * un + u) * 8, 8) for u in range(un)]
            new = [ok / (6.0 + rb[p, pl.ds(y, 8), :]) for y in ys]
            for y, v in zip(ys, new):
                rb[p, pl.ds(y, 8), :] = v
            return c

        return lax.fori_loop(0, tiles // un, block, carry)

    lax.fori_loop(1, 15, invert, 0)
    edges(rb)
    last = iota((8, 128), 1) == 127
    apart = jnp.abs(iota((128, 128), 0) - iota((128, 128), 1))
    shifts = jnp.where(apart == 1, 1.0, 0.0).astype(BF16)
    shifts = jnp.concatenate([shifts, shifts], axis=0)

    def sweep(buf, k, begin, count, store):
        w = sweep_weight(k)

        def pair(q, carry):
            p = k + 1 + 2 * q
            for i in MXU_PLANES:
                c = buf[p + i, begin : begin + 8 * count, :]
                head = c.astype(BF16)
                tail = (c - head.astype(F32)).astype(BF16)
                both = jnp.concatenate([head, tail], axis=1)
                zb[i, : 8 * count, :] = jnp.dot(both, shifts, preferred_element_type=F32)
            for t in range(count):
                y = begin + 8 * t
                v = [buf[p - 1 + i, y : y + 8, :] for i in range(4)]
                for i in range(2):
                    ym = buf[p + i, y - 1 : y + 7, :]
                    yp = buf[p + i, y + 1 : y + 9, :]
                    if i in MXU_PLANES:
                        zs = zb[i, 8 * t : 8 * t + 8, :]
                    else:
                        zr = jnp.where(last, 0.0, pltpu.roll(v[i + 1], 127, axis=1))
                        zs = pltpu.roll(v[i + 1], 1, axis=1) + zr
                    nb = ((v[i] + v[i + 2]) + (ym + yp)) + zs
                    store(p + i, y, ((1.0 - w) / w) * v[i + 1] + rb[p + i, y : y + 8, :] * nb)
            return carry

        lax.fori_loop(0, 7 - k, pair, 0)

    def into(buf):
        def store(p, y, new):
            buf[p, y : y + 8, :] = new

        return store

    scale = -math.prod(sweep_weight(k) for k in range(SWEEPS)) ** 2

    def product(p, y, new):
        out[p - 4, y - 16 : y - 8, :] = (scale * f0[p, y : y + 8, :]) * new

    for bufs, cps in (((f0, f1), f_cps), ((a0, a1), a_cps)):
        for cp in cps:
            cp.wait()
        for k in range(SWEEPS):
            src, dst = bufs[k % 2], bufs[1 - k % 2]
            if k < SWEEPS - 1:
                sweep(src, k, 8, tiles, into(dst))
            elif src is f1:
                sweep(src, k, 16, rows // 8, into(dst))
            else:
                sweep(src, k, 16, rows // 8, product)


def deep_call(meta, fwd, adj, absn, near, far, chunk):
    sends, offset, rows = chunk
    ny = fwd.shape[1]
    any_spec = pl.BlockSpec(memory_space=pl.ANY)
    return pl.pallas_call(
        functools.partial(deep_kernel, sends=sends, offset=offset, rows=rows, ny=ny),
        out_shape=jax.ShapeDtypeStruct((8, rows, 128), F32),
        in_specs=[pl.BlockSpec(memory_space=pltpu.SMEM)] + [any_spec] * 5,
        out_specs=pl.BlockSpec(memory_space=pltpu.VMEM),
        scratch_shapes=[
            pltpu.VMEM((16, rows + 32, 128), F32),
            pltpu.VMEM((16, rows + 32, 128), F32),
            pltpu.VMEM((16, rows + 32, 128), F32),
            pltpu.VMEM((16, rows + 32, 128), F32),
            pltpu.VMEM((16, rows + 32, 128), F32),
            pltpu.VMEM((2, rows + 16, 128), F32),
            pltpu.SemaphoreType.DMA((3, 3)),
        ],
    )(meta, fwd, adj, absn, near, far)


def final_kernel(*refs, n_own, n_got):
    own = refs[:n_own]
    got = refs[n_own : n_own + n_got]
    keep, recv, out, packed = refs[n_own + n_got :]
    x = pl.program_id(0)

    @pl.when(x == 0)
    def _():
        both = keep[...] + recv[...]
        for v in range(both.shape[1] // 128):
            cols = both[:, 128 * v : 128 * v + 128]
            cols = jnp.concatenate([cols, cols], axis=0)
            packed[128 * v : 128 * v + 128, :] = cols.T

    def cover(parts):
        at = 0
        found = []
        for ref in parts:
            found.append((at, ref.shape[1], ref))
            at += ref.shape[1]
        return found

    cuts = sorted({a for a, _, _ in cover(own)} | {a for a, _, _ in cover(got)} | {out.shape[1]})

    def piece(parts, a, b, i):
        for at, size, ref in cover(parts):
            if at <= a and b <= at + size:
                return ref[i, a - at : b - at, :]

    for a, b in zip(cuts[:-1], cuts[1:]):
        for i in range(PLANES):
            shift = (128 - 8 * (PLANES * x + i)) % 128
            shallow = pltpu.roll(packed[a:b, :], shift, axis=1)
            deep = piece(own, a, b, i) + piece(got, a, b, i)
            out[i, a:b, :] = jnp.where(iota((b - a, 128), 1) < 4, shallow, deep)


def final_call(own, got, keep, recv):
    half = keep.shape[1]

    def spec(a):
        return pl.BlockSpec((PLANES, a.shape[1], 128), lambda x: (x, 0, 0))

    whole = pl.BlockSpec((64, half), lambda x: (0, 0))
    return pl.pallas_call(
        functools.partial(final_kernel, n_own=len(own), n_got=len(got)),
        out_shape=jax.ShapeDtypeStruct((8, half, 128), F32),
        grid=(8 // PLANES,),
        in_specs=[spec(a) for a in own + got] + [whole, whole],
        out_specs=pl.BlockSpec((PLANES, half, 128), lambda x: (x, 0, 0)),
        scratch_shapes=[pltpu.VMEM((half, 128), F32)],
        name="final",
    )(*own, *got, keep, recv)


def after(value, *others):
    return lax.optimization_barrier((value, others))[0]


def shards(pattern_index, patterns, freq_bins, absorption, forward_start, adjoint_start, measured):
    ny = forward_start.shape[2]
    parts = lax.axis_size(GX)
    total_x = parts * 8
    fwd = forward_start[0]
    adj = adjoint_start[0]
    gx = lax.axis_index(GX)
    meta = jnp.stack(
        [
            lax.axis_index("pat"),
            (gx > 0).astype(jnp.int32),
            (gx < parts - 1).astype(jnp.int32),
            pattern_index[0],
            gx % 2,
        ]
    ).astype(jnp.int32)

    lid = [[p * parts + g for g in range(parts)] for p in range(2)]
    near_pairs = [(r[g], r[g ^ 1]) for r in lid for g in range(parts)]
    far_pairs = []
    for r in lid:
        for g in range(1, parts - 1, 2):
            far_pairs += [(r[g], r[g + 1]), (r[g + 1], r[g])]
    pat_pairs = [(lid[p][g], lid[1 - p][g]) for p in range(2) for g in range(parts)]

    def exchange(near, far):
        near = lax.ppermute(near, ALL, near_pairs)
        far = lax.ppermute(far, ALL, far_pairs)
        return near, far

    out = head_call(meta, fwd, adj, absorption, patterns, CHUNKS[:EARLY])
    t1, t2, src, near, far = out[2 * EARLY :]
    near, far = exchange(near, far)
    halos = [exchange(out[2 * c], out[2 * c + 1]) for c in range(EARLY)]
    meta = after(meta, t1)

    def table(phase):
        angle = 2.0 * math.pi / total_x * (phase % total_x).astype(F32)
        scale = math.sqrt(total_x)
        return jnp.cos(angle) / scale, -(jnp.sin(angle) / scale)

    bins = after(freq_bins, meta)
    x_at = jnp.arange(parts, dtype=jnp.int32) * 8
    x_in = jnp.arange(8, dtype=jnp.int32)[:, None] + x_at[None, :]
    x_out = (jnp.arange(-4, 12, dtype=jnp.int32)[:, None] + x_at[None, :]).reshape(-1)
    to_data = jnp.concatenate(table(bins[None, :, None] * x_in[:, None, :]), axis=1)
    to_data = to_data.reshape(8 * 32, parts)
    from_data = jnp.concatenate(table(bins[:, None] * x_out[None, :]), axis=0)
    seen = measured.reshape(32, 16)
    meta = after(meta, to_data, from_data)

    own, arrived = [], []

    def deep(meta, c):
        terms = deep_call(meta, fwd, adj, absorption, *halos[c], CHUNKS[c])
        if CHUNKS[c][0]:
            arrived.append(lax.ppermute(terms, ALL, pat_pairs))
        else:
            own.append(terms)
        return after(meta, terms)

    fsh, surf, *faces = forward_call(
        meta, t1, t2, src, near, far, fwd, adj, absorption, CHUNKS[EARLY:]
    )
    meta = after(meta, surf)
    got = lax.all_to_all(surf, GX, 0, 0, tiled=True)
    for c in range(EARLY, len(CHUNKS)):
        at = 2 * (c - EARLY)
        halos.append(exchange(faces[at], faces[at + 1]))
    meta = deep(meta, 0)
    model, rows = vmem_call(
        data_kernel, [(32, 128), (parts, 256)], [pltpu.VMEM((32, 128), F32)], 4
    )(meta, got, to_data, from_data, seen)
    meta = after(meta, rows)
    back = lax.all_to_all(rows, GX, 0, 0, tiled=True)
    for c in range(1, len(CHUNKS)):
        meta = deep(meta, c)
    send, keep = vmem_call(
        functools.partial(adjoint_kernel, ny=ny),
        [(64, ny // 2), (64, ny // 2)],
        shallow_scratch(ny) + [pltpu.VMEM((64, ny), F32)],
        6,
    )(meta, t1, t2, back, near, far, fsh)
    recv = lax.ppermute(send, ALL, pat_pairs)
    gradient = final_call(own, arrived, keep, recv)
    return (gradient, model[:, :16].reshape(1, 2, 16, 16))


def solution(mesh):
    torus = Mesh(mesh.devices.reshape(mesh.shape["pat"], 4, 2, 4, 2), ALL)
    in_specs = (
        P("pat"),
        P(None, GX, None),
        P(),
        P(GX, None, None),
        P("pat", GX, None, None),
        P("pat", GX, None, None),
        P("pat", None, None, GX),
    )
    out_specs = (P(GX, "pat", None), P("pat", None, None, GX))

    return jax.shard_map(
        shards, mesh=torus, in_specs=in_specs, out_specs=out_specs, check_vma=False
    )
```
